32 devices in a mesh: group: 2 (over y), ctx: 8 (over z, core), head: 2 (over x).
Axes of the slice: x: 2, y: 2, z: 4, core: 2. Of those that a mesh axis runs over, the one named last changes fastest.
Arguments:
- queries: bfloat16 [2048, 4096], P(('group', 'ctx'), 'head'), parts along dimension 0, may hold values from -6 to 6
- keys: bfloat16 [2048, 512], P(('group', 'ctx'), 'head'), parts along dimension 0, may hold values from -6 to 6
- values: bfloat16 [2048, 512], P(('group', 'ctx'), 'head'), parts along dimension 0, may hold values from -6 to 6
- sinks: float32 [64], P('head'), may hold values from 0 to 4
- segments: int32 [2048], P('group'), parts along dimension 0, may hold values from 0 to 3, never falling along the last dimension, each value on 1 to 768 neighbouring positions
- hidden_in: bfloat16 [2048, 2880], P(('group', 'ctx')), parts along dimension 0, may hold values from -6 to 6
- routes: int32 [2048, 4], P(('group', 'ctx')), parts along dimension 0, may hold values from 0 to 7, all different within a row; in each aligned block of 64 rows (0 to 63, 64 to 127, ...) at most 48 rows name the same one
- w_out: bfloat16 [4096, 2880], P('head'), may hold values from -0.09375 to 0.09375
- norm_gain: float32 [2880], replicated, may hold values from 0.1 to 1.9
- router: bfloat16 [2880, 8], replicated, may hold values from -0.109375 to 0.109375
- w_gate_up: bfloat16 [8, 2, 2880, 2880], P('ctx', None, None, 'head'), may hold values from -0.109375 to 0.109375
- w_down: bfloat16 [8, 2880, 2880], P('ctx', 'head'), may hold values from -0.109375 to 0.109375
Outputs:
- layer_out: bfloat16 [2048, 2880], P(('group', 'ctx', 'head')), parts along dimension 0
The draws below stay inside these ranges and needn't reach their ends.
There are 2 independent parts, one for each index of `group`. The reference program is written for one: setup_inputs(seed, part) draws one part's arguments, and reference() takes and returns one part's arrays. A program takes and returns all parts, laid end to end along the dimension named above; an argument that names none is the same for every part. Nothing has to cross between parts.
Inputs may be any that keep to these rules, and one draw needn't show every extreme that they name: `routes`: each row names 4 different experts; in each aligned block of 64 rows no expert is named by more than 48 rows, a bound that some block reaches. `segments`: requests fill consecutive positions in order; the longest has 768 positions.
All inputs are finite; a program needn't handle non-finite values.
Results may differ from the reference program's by a relative error of at most 0.015.
Values may be sent and summed in bfloat16 or wider, within the bound.
A program may use at most 128 MiB of HBM per device.

```python
import math
import jax
import jax.numpy as jnp
import numpy as np
from jax import lax

D = 2880
QUERY_HEADS = 64
KEY_VALUE_HEADS = 8
HEAD_SIZE = 64
FF = 2880
TOPK = 4
TOTAL_POSITIONS = 1024
EXPERTS = 8
ROWS_DEV = 64
CAP = 48
SLICE = 1440
N_CTX = 8
N_HEAD = 2


def query_key_pair(key):
    first, second_choice = jax.random.split(key, 2)
    queries = jnp.clip(jax.random.normal(first, (TOTAL_POSITIONS, QUERY_HEADS * HEAD_SIZE), jnp.float32), -6.0, 6.0)
    keys = jnp.clip(jax.random.normal(second_choice, (TOTAL_POSITIONS, KEY_VALUE_HEADS * HEAD_SIZE), jnp.float32), -6.0, 6.0)
    return (queries, keys)


def draw_queries(key, part):
    return query_key_pair(key)[0].astype(jnp.bfloat16)


def draw_keys(key, part):
    return query_key_pair(key)[1].astype(jnp.bfloat16)


def shard_levels(own_key, shape, cuts, smallest, top_value):
    def one(dim, blocks):
        steps = jax.random.uniform(jax.random.fold_in(jax.random.fold_in(own_key, 6), dim), (blocks,), jnp.float32, smallest / len(cuts), top_value / len(cuts))
        return jnp.repeat(jnp.exp(steps), shape[dim] // blocks).reshape((-1,) + (1,) * (len(shape) - dim - 1))

    loudness = one(*cuts[0])
    for cut in cuts[1:]:
        loudness = loudness * one(*cut)
    return loudness


def split_up(count, total, reach, skew):
    portions = [(1 << 20) // math.isqrt(rank ** skew) + 1 for rank in range(2, count + 1)]
    surplus, holding = total - reach - (count - 1), [1] * (count - 1)
    while surplus > 0:
        free = [i for i in range(count - 1) if holding[i] < reach]
        whole, left = sum([portions[i] for i in free]), surplus
        for i in free:
            addition = min(reach - holding[i], max(1, left * portions[i] // whole), surplus)
            holding[i] = holding[i] + addition
            surplus = surplus - addition
    return np.array([reach] + holding)


def uneven_parts(stream_key, count, total, bound, skew):
    if count == 2:
        one = jax.random.randint(stream_key, (), max(1, total - bound), min(bound, total - 1) + 1)
        return jnp.stack([one, total - one])
    tallies = jnp.asarray(split_up(count, total, bound, skew), jnp.int32)
    twos = (count - 1) // 2
    donor, taker = tallies[1:1 + 2 * twos:2], tallies[2:2 + 2 * twos:2]
    margin = jnp.minimum(donor - 1, bound - taker)
    passed = jax.random.randint(jax.random.fold_in(stream_key, 1), (twos,), 0, 1 << 20) % (margin + 1)
    tallies = tallies.at[1:1 + 2 * twos:2].set(donor - passed).at[2:2 + 2 * twos:2].set(taker + passed)
    return tallies[jax.random.permutation(jax.random.fold_in(stream_key, 2), count)]


def deal_out(stream_key, own, number, rows, amount, top, limit, lean):
    ranking = jax.random.permutation(stream_key, amount)
    heavy_load, usual = load_shares(amount, rows * top, limit, lean, True), load_shares(amount, rows * top, limit, lean, False)
    places = jnp.arange(amount)

    def named(tallies, offset_by):
        used = int((tallies > 0).sum())
        fixed = max(1, used // 4)
        shifted = fixed + (places - fixed + offset_by * (used - fixed)) % max(1, amount - fixed)
        return jnp.zeros((amount,), jnp.int32).at[ranking[jnp.where(places < fixed, places, shifted)]].set(jnp.asarray(tallies, jnp.int32))

    tallies = jnp.where(number % 4 == 0, named(heavy_load, number // 4), named(usual, number - number // 4 - 1))
    mixed = jax.random.permutation(jax.random.fold_in(own, 3), amount)
    source_of, receiver = mixed[0:amount // 2 * 2:2], mixed[1:amount // 2 * 2:2]
    slack = jnp.minimum(tallies[source_of] - 1, limit - tallies[receiver]) // 2
    slack = jnp.where((source_of == ranking[0]) | (receiver == ranking[0]) | (tallies[receiver] == 0), 0, jnp.maximum(slack, 0))
    shifted = jax.random.randint(jax.random.fold_in(own, 4), (amount // 2,), 0, 1 << 20) % (slack + 1)
    tallies = tallies.at[source_of].add(-shifted).at[receiver].add(shifted)
    labels = jnp.searchsorted(jnp.cumsum(tallies), jnp.arange(rows * top), side="right").astype(jnp.int32)
    table = labels.reshape(top, rows).T
    table = table[jax.random.permutation(jax.random.fold_in(own, 1), rows)]
    offset_by = jax.random.randint(jax.random.fold_in(own, 2), (rows, 1), 0, top)
    return jnp.take_along_axis(table, (jnp.arange(top)[None, :] + offset_by) % top, axis=1)


def load_shares(amount, total, most, skew, full):
    portions = [(1 << 20) // math.isqrt(grade ** skew) + 1 for grade in range(1, amount + 1)]
    largest = most if full else min(most, max(-(-total // amount), total * portions[0] // sum(portions)))
    least = 1 if total - largest >= amount - 1 else 0
    counts, rest = [largest] + [least] * (amount - 1), total - largest - least * (amount - 1)
    while rest > 0:
        candidates = [i for i in range(1, amount) if counts[i] < largest] or [i for i in range(1, amount) if counts[i] < most]
        whole, remaining = sum([portions[i] for i in candidates]), rest
        for i in candidates:
            addition = min(most - counts[i], max(1, remaining * portions[i] // whole), rest)
            counts[i] = counts[i] + addition
            rest = rest - addition
    return np.array(counts)


def bell_draw(rng, extent, width, most, cuts=(), kind=jnp.bfloat16):
    values = jax.random.normal(rng, extent, jnp.float32) * width
    if len(cuts) > 0:
        values = shard_levels(rng, extent, cuts, -0.22, 0.18) * values
    return jnp.clip(values, min=-most, max=most).astype(kind)


def setup_inputs(seed: int = 0, part: int = 0) -> dict:
    key_of = jax.random.split(jax.random.key(seed), 13)
    part_keys = jax.random.split(jax.random.fold_in(key_of[12], part), 13)
    queries = draw_queries(jax.random.fold_in(jax.random.fold_in(key_of[12], part), 71), part)
    keys = draw_keys(jax.random.fold_in(jax.random.fold_in(key_of[12], part), 71), part)
    values = bell_draw(part_keys[2], (TOTAL_POSITIONS, KEY_VALUE_HEADS * HEAD_SIZE), 1.0, 6.0, ((0, 8), (1, 2)))
    sinks = jnp.clip(4.0 * jax.random.uniform(key_of[3], (QUERY_HEADS,), jnp.float32) ** shard_levels(key_of[3], (QUERY_HEADS,), ((0, 2),), -0.2, 0.2), 0.0, 4.0)
    segments = jnp.searchsorted(jnp.cumsum(uneven_parts(part_keys[4], 4, TOTAL_POSITIONS, 3 * TOTAL_POSITIONS // 4, 0)), jnp.arange(TOTAL_POSITIONS), side="right").astype(jnp.int32)
    hidden_in = bell_draw(part_keys[5], (TOTAL_POSITIONS, D), 1.0, 6.0, ((0, 8),))
    routes_keys = jax.random.split(jax.random.fold_in(part_keys[6], 1), TOTAL_POSITIONS // ROWS_DEV)
    routes_turns = jax.random.permutation(jax.random.fold_in(part_keys[6], 3), TOTAL_POSITIONS // ROWS_DEV)
    routes = jax.vmap(lambda own, number: deal_out(jax.random.fold_in(part_keys[6], 2), own, number, ROWS_DEV, EXPERTS, TOPK, CAP, 2))(routes_keys, routes_turns).reshape((TOTAL_POSITIONS, TOPK))
    w_out = bell_draw(key_of[7], (QUERY_HEADS * HEAD_SIZE, D), (QUERY_HEADS * HEAD_SIZE) ** -0.5, 0.09375, ((0, 2),))
    norm_gain = jnp.clip(1.0 + 0.18 * jax.random.normal(key_of[8], (D,), jnp.float32), 0.1, 1.9)
    router = bell_draw(key_of[9], (D, EXPERTS), D ** -0.5, 0.109375)
    w_gate_up = bell_draw(key_of[10], (EXPERTS, 2, D, FF), D ** -0.5, 0.109375, ((0, 8), (3, 2)))
    w_down = bell_draw(key_of[11], (EXPERTS, FF, D), FF ** -0.5, 0.109375, ((0, 8), (1, 2)))
    return {"queries": queries, "keys": keys, "values": values, "sinks": sinks, "segments": segments, "hidden_in": hidden_in, "routes": routes, "w_out": w_out, "norm_gain": norm_gain, "router": router, "w_gate_up": w_gate_up, "w_down": w_down}


masked_value = -1e+30

def reference(queries, keys, values, sinks, segments, hidden_in, routes, w_out, norm_gain, router, w_gate_up, w_down):
    group_share = QUERY_HEADS // KEY_VALUE_HEADS
    positions = jnp.arange(TOTAL_POSITIONS, dtype=jnp.int32)
    visible = (positions[None, :] <= positions[:, None]) & (segments[None, :] == segments[:, None])

    def key_value_share(kv_index):
        query_part = lax.dynamic_slice_in_dim(queries, kv_index * group_share * HEAD_SIZE, group_share * HEAD_SIZE, 1)
        query_part = query_part.reshape(TOTAL_POSITIONS, group_share, HEAD_SIZE).astype(jnp.float32)
        key_part = lax.dynamic_slice_in_dim(keys, kv_index * HEAD_SIZE, HEAD_SIZE, 1).astype(jnp.float32)
        value_part = lax.dynamic_slice_in_dim(values, kv_index * HEAD_SIZE, HEAD_SIZE, 1).astype(jnp.float32)
        sink_part = lax.dynamic_slice_in_dim(sinks, kv_index * group_share, group_share, 0)
        scores = jnp.einsum('tgd,nd->gtn', query_part, key_part) * HEAD_SIZE ** (-0.5)
        scores = jnp.where(visible[None], scores, masked_value)
        top_score = jnp.maximum(sink_part[:, None], lax.optimization_barrier(jnp.max(scores, axis=-1)))
        probs = jnp.where(visible[None], jnp.exp(scores - top_score[..., None]), 0.0)
        denom = lax.optimization_barrier(jnp.sum(probs, axis=-1)) + jnp.exp(sink_part[:, None] - top_score)
        probs_b = lax.optimization_barrier(probs.astype(jnp.bfloat16)).astype(jnp.float32)
        attended = jnp.einsum('gtn,nd->gtd', probs_b, value_part) / denom[..., None]
        return attended.astype(jnp.bfloat16).transpose(1, 0, 2)
    head_share = lax.map(key_value_share, jnp.arange(KEY_VALUE_HEADS, dtype=jnp.int32))
    attended = head_share.transpose(1, 0, 2, 3).reshape(TOTAL_POSITIONS, QUERY_HEADS * HEAD_SIZE)
    projected = jnp.dot(attended, w_out, preferred_element_type=jnp.float32)
    residual = (hidden_in.astype(jnp.float32) + projected).astype(jnp.bfloat16)
    widened = residual.astype(jnp.float32)
    normed = (widened * lax.rsqrt(lax.optimization_barrier(jnp.mean(widened * widened, axis=-1, keepdims=True)) + 1e-05) * norm_gain).astype(jnp.bfloat16)
    logits = jnp.dot(normed, router, preferred_element_type=jnp.float32)
    gates = jax.nn.softmax(jnp.take_along_axis(logits, routes, axis=1), axis=-1)
    rows_max = min(TOTAL_POSITIONS, N_CTX * N_HEAD * CAP)
    token_index = jnp.arange(TOTAL_POSITIONS, dtype=jnp.int32)

    def per_expert(carried, expert):
        chosen = routes == expert
        selected = jnp.any(chosen, axis=1)
        weight = lax.optimization_barrier(jnp.sum(jnp.where(chosen, gates, 0.0), axis=1))
        order_key = jnp.where(selected, token_index, TOTAL_POSITIONS + token_index)
        taken = jnp.argsort(order_key)[:rows_max].astype(jnp.int32)
        token_rows = normed[taken]
        gate_up = lax.dynamic_index_in_dim(w_gate_up, expert, 0, keepdims=False)
        down_full = lax.dynamic_index_in_dim(w_down, expert, 0, keepdims=False)
        gate_pre = jnp.dot(token_rows, gate_up[0], preferred_element_type=jnp.float32)
        up_pre = jnp.dot(token_rows, gate_up[1], preferred_element_type=jnp.float32)
        activation = (gate_pre * jax.nn.sigmoid(1.702 * gate_pre) * (up_pre + 1.0)).astype(jnp.bfloat16)
        act_slices = activation.reshape(rows_max, N_HEAD, SLICE).astype(jnp.float32)
        down_slices = down_full.reshape(N_HEAD, SLICE, D).astype(jnp.float32)
        pieces = jnp.einsum('msf,sfd->smd', act_slices, down_slices).astype(jnp.bfloat16)
        pieces = lax.optimization_barrier(pieces)
        expert_out = lax.optimization_barrier(jnp.sum(pieces.astype(jnp.float32), axis=0)).astype(jnp.bfloat16)
        contrib = weight[taken][:, None] * expert_out.astype(jnp.float32)
        return (carried.at[taken].add(contrib), None)
    mixture, _ = lax.scan(per_expert, jnp.zeros((TOTAL_POSITIONS, D), jnp.float32), jnp.arange(EXPERTS, dtype=jnp.int32))
    return (residual.astype(jnp.float32) + mixture).astype(jnp.bfloat16)
```

```python
import functools

import jax
import jax.numpy as jnp
from jax import lax
from jax.experimental import pallas as pl
from jax.experimental.pallas import tpu as pltpu
from jax.sharding import PartitionSpec as P

HEAD_SIZE = 64


masked_value = -1e30


def attend_kernel(
    query_ref, key_ref, value_ref, sink_ref, place_ref, segment_ref, own_segment_ref, out_ref
):
    rows = query_ref.shape[0]
    kv_groups = key_ref.shape[1] // HEAD_SIZE
    share = query_ref.shape[1] // key_ref.shape[1]
    spot = lax.broadcasted_iota(jnp.int32, (rows, key_ref.shape[0]), 1)
    visible = (spot <= place_ref[...]) & (segment_ref[...] == own_segment_ref[...])
    hidden_bias = jnp.where(visible, 0.0, masked_value)
    for group in range(kv_groups):
        span = slice(group * HEAD_SIZE, (group + 1) * HEAD_SIZE)
        group_keys = key_ref[:, span]
        group_values = value_ref[:, span]
        for pair in range(share // 2):
            both = []
            for member in range(2):
                head = group * share + pair * 2 + member
                query = query_ref[:, head * HEAD_SIZE : (head + 1) * HEAD_SIZE]
                scores = lax.dot_general(
                    query, group_keys, (((1,), (1,)), ((), ())), preferred_element_type=jnp.float32
                )
                scores = scores * HEAD_SIZE ** (-0.5) + hidden_bias
                sink = sink_ref[:, head : head + 1]
                top = jnp.maximum(jnp.max(scores, axis=-1, keepdims=True), sink)
                weights = jnp.exp(scores - top)
                total = jnp.sum(weights, axis=-1, keepdims=True) + jnp.exp(sink - top)
                mixed = jnp.dot(weights.astype(jnp.bfloat16), group_values, preferred_element_type=jnp.float32)
                both.append((mixed / total).astype(jnp.bfloat16))
            first = (group * share + pair * 2) * HEAD_SIZE
            out_ref[:, first : first + 2 * HEAD_SIZE] = jnp.concatenate(both, axis=1)


def attend(queries, all_keys, all_values, sinks, tok_pos, tok_seg, segments):
    return pl.pallas_call(
        attend_kernel,
        out_shape=jax.ShapeDtypeStruct(queries.shape, jnp.bfloat16),
        in_specs=[full_vmem()] * 7,
        out_specs=full_vmem(),
        name="attend",
    )(
        queries,
        all_keys,
        all_values,
        sinks.reshape(1, -1),
        tok_pos.reshape(-1, 1),
        segments.reshape(1, -1),
        tok_seg.reshape(-1, 1),
    )


MESH = pl.DeviceIdType.MESH
LANES = 128
CORES = 2


def full_vmem():
    return pl.BlockSpec(memory_space=pltpu.VMEM)


class Ring:
    def __init__(self, chips, heads):
        self.chips, self.heads, self.count = chips, heads, chips * heads
        ctx = lax.axis_index("ctx")
        self.head = lax.axis_index("head")
        self.core = lax.rem(ctx, CORES)
        z = lax.div(ctx, CORES)
        self.place = self.head * chips + z + lax.rem(self.head, 2) * (chips - 1 - 2 * z)
        self.partner = {"ctx": z * CORES + 1 - self.core, "head": self.head}

    def at(self, offset):
        spot = lax.rem(self.place + offset + self.count, self.count)
        head = lax.div(spot, self.chips)
        step = lax.rem(spot, self.chips)
        return head, step + lax.rem(head, 2) * (self.chips - 1 - 2 * step)

    def block(self, offset, core):
        head, z = self.at(offset)
        return (z * CORES + core) * self.heads + head

    def device(self, offset):
        head, z = self.at(offset)
        return {"ctx": z * CORES + self.core, "head": head}


def remote(src, dst, send_sem, recv_sem, device):
    return pltpu.make_async_remote_copy(
        src_ref=src, dst_ref=dst, send_sem=send_sem, recv_sem=recv_sem, device_id=device, device_id_type=MESH
    )


def greet(devices):
    barrier = pltpu.get_barrier_semaphore()
    for device in devices:
        pl.semaphore_signal(barrier, inc=1, device_id=device, device_id_type=MESH)
    pl.semaphore_wait(barrier, len(devices))


def row_chunks(rows):
    if rows % 32 == 0:
        return [pl.ds(0, rows // 2), pl.ds(rows // 2, rows // 2)]
    return [pl.ds(0, rows)]


def line_kernel(chips, key_ref, value_ref, all_keys, all_values, line_send, line_recv, pair_send, pair_recv, own_sem):
    ctx = lax.axis_index("ctx")
    z, core = lax.div(ctx, CORES), lax.rem(ctx, CORES)
    ins, outs = (key_ref, value_ref), (all_keys, all_values)
    partner = {"ctx": z * CORES + 1 - core}
    ways = ((0, 1), (1, -1))

    def inside(spot):
        return (spot >= 0) & (spot < chips)

    barrier = pltpu.get_barrier_semaphore()
    pl.semaphore_signal(barrier, inc=1, device_id=partner, device_id_type=MESH)
    for _, way in ways:

        @pl.when(inside(z + way))
        def _():
            pl.semaphore_signal(
                barrier, inc=1, device_id={"ctx": (z + way) * CORES + core}, device_id_type=MESH
            )

    peers = 1 + sum(jnp.where(inside(z + way), 1, 0) for _, way in ways)
    pl.semaphore_wait(barrier, peers)

    def hop(index, way, step, part):
        block = (z - way * step) * CORES + core
        source = ins[part] if step == 0 else outs[part].at[block]
        return remote(
            source,
            outs[part].at[block],
            line_send.at[index, step, part],
            line_recv.at[index, step, part],
            {"ctx": (z + way) * CORES + core},
        )

    def share(slot, block, part):
        source = ins[part] if slot == 0 else outs[part].at[block]
        return remote(source, outs[part].at[block], pair_send.at[slot, part], pair_recv.at[slot, part], partner)

    def keep(part):
        return pltpu.make_async_copy(ins[part], outs[part].at[ctx], own_sem.at[part])

    for part in (0, 1):
        for index, way in ways:

            @pl.when(inside(z + way))
            def _():
                hop(index, way, 0, part).start()

    for part in (0, 1):
        share(0, ctx, part).start()
        keep(part).start()
    for step in range(1, chips):
        for part in (0, 1):
            for index, way in ways:

                @pl.when(inside(z - way * step))
                def _():
                    hop(index, way, step - 1, part).wait_recv()
                    if step < chips - 1:

                        @pl.when(inside(z + way))
                        def _():
                            hop(index, way, step, part).start()

                    share(index * (chips - 1) + step, (z - way * step) * CORES + core, part).start()

    for part in (0, 1):
        keep(part).wait()
        share(0, ctx, part).wait()
        for index, way in ways:
            for step in range(chips):
                if step < chips - 1:

                    @pl.when(inside(z + way) & inside(z - way * step))
                    def _():
                        hop(index, way, step, part).wait_send()

                if step > 0:

                    @pl.when(inside(z - way * step))
                    def _():
                        share(index * (chips - 1) + step, (z - way * step) * CORES + core, part).wait()


def gather_keys(keys, values):
    n_ctx = lax.axis_size("ctx")
    chips = n_ctx // CORES
    shape = jax.ShapeDtypeStruct((n_ctx,) + keys.shape, keys.dtype)
    slots = 2 * (chips - 1) + 1
    gathered = pl.pallas_call(
        functools.partial(line_kernel, chips),
        out_shape=(shape, shape),
        in_specs=[full_vmem()] * 2,
        out_specs=(full_vmem(),) * 2,
        scratch_shapes=[
            pltpu.SemaphoreType.DMA((2, chips, 2)),
            pltpu.SemaphoreType.DMA((2, chips, 2)),
            pltpu.SemaphoreType.DMA((slots, 2)),
            pltpu.SemaphoreType.DMA((slots, 2)),
            pltpu.SemaphoreType.DMA((2,)),
        ],
        compiler_params=pltpu.CompilerParams(collective_id=0, has_side_effects=True),
        name="gather_keys",
    )(keys, values)
    return [array.reshape(-1, array.shape[-1]) for array in gathered]


def layer_kernel(
    chips, heads, experts, capacity, tile, columns, part_ref, hidden_ref, gain_ref, router_ref, route_ref, up_hbm, down_hbm,
    out_ref, all_ref, residual_ref, hidden_rows, route_rows, lanes_ref, slots, up_ref, down_ref, rows_ref, act_ref,
    gate_ref, back_ref, term_ref, got, outgoing, incoming, weight_sem, head_send, head_recv,
    hop_send, hop_recv, copy_send, copy_recv, pair_send, pair_recv, ring_send, ring_recv,
):
    ring = Ring(chips, heads)
    count, half = ring.count, ring.count // 2
    rows, width = out_ref.shape
    start = width % LANES
    chunks = row_chunks(rows)
    parts = range(len(chunks))
    ways = ((0, 1), (1, -1))
    turned = (((1,), (1,)), ((), ()))
    ctx, head = lax.axis_index("ctx"), ring.head
    others = [{"ctx": ctx, "head": lax.rem(head + turn, heads)} for turn in range(1, heads)]

    greet([ring.device(1), ring.device(-1), ring.partner] + others)
    sends = []
    for turn, device in enumerate(others):
        target = pl.ds(pl.multiple_of(device["head"] * rows, rows), rows)
        copy = remote(part_ref.at[target], slots.at[turn], head_send.at[turn], head_recv.at[turn], device)
        copy.start()
        sends.append(copy)

    loads = [
        pltpu.make_async_copy(up_hbm, up_ref, weight_sem.at[0]),
        pltpu.make_async_copy(down_hbm, down_ref, weight_sem.at[1]),
    ]
    for copy in loads:
        copy.start()

    own = pl.ds(pl.multiple_of(head * rows, rows), rows)
    hidden_rows[...] = hidden_ref[...].T
    tokens = route_ref.shape[1]
    eye = (
        lax.broadcasted_iota(jnp.int32, (tokens, tokens), 0) == lax.broadcasted_iota(jnp.int32, (tokens, tokens), 1)
    ).astype(jnp.float32)
    route_rows[...] = lax.dot_general(
        eye.astype(jnp.bfloat16),
        route_ref[...].astype(jnp.float32).astype(jnp.bfloat16),
        turned,
        preferred_element_type=jnp.float32,
    )
    lanes_ref[...] = jnp.zeros(lanes_ref.shape, lanes_ref.dtype)
    lanes_ref[start : start + experts, :] = router_ref[...]
    lanes_ref[start + experts : start + 2 * experts, :] = router_ref[...]

    total = hidden_rows[own, :].astype(jnp.float32) + part_ref[own, :].astype(jnp.float32)
    for turn, copy in enumerate(sends):
        copy.wait_recv()
        total = total + slots[turn].astype(jnp.float32)
    residual = total.astype(jnp.bfloat16)
    residual_ref[...] = residual
    wide = residual.astype(jnp.float32)
    scale = lax.rsqrt(jnp.mean(wide * wide, axis=-1, keepdims=True) + 1e-05)
    normed = (wide * scale * gain_ref[...]).astype(jnp.bfloat16)

    logits = lax.dot_general(normed, lanes_ref[...], turned, preferred_element_type=jnp.float32)
    lane = lax.broadcasted_iota(jnp.int32, logits.shape, 1) - start
    first = (lane >= 0) & (lane < experts)
    third = (lane >= 2 * experts) & (lane < 3 * experts)
    names = route_rows[own, :]
    present = jnp.zeros(logits.shape, jnp.bool_)
    named = jnp.zeros(logits.shape, jnp.bool_)
    spot = lane.astype(jnp.float32)
    for k in range(route_ref.shape[0]):
        name = names[:, k : k + 1]
        present = present | (spot == name) | (spot - experts == name)
        named = named | (spot - 2 * experts == name)
    top = jnp.max(jnp.where(present, logits, -jnp.inf), axis=-1, keepdims=True)
    powers = jnp.where(present, jnp.exp(jnp.where(present, logits - top, 0.0)), 0.0)
    gates = powers / jnp.sum(jnp.where(first, powers, 0.0), axis=-1, keepdims=True)
    coarse = gates.astype(jnp.bfloat16)
    rest = gates - coarse.astype(jnp.float32)
    earlier = lax.broadcasted_iota(jnp.int32, (rows, rows), 0) > lax.broadcasted_iota(jnp.int32, (rows, rows), 1)
    rank = jnp.dot(
        earlier.astype(jnp.float32).astype(jnp.bfloat16),
        named.astype(jnp.float32).astype(jnp.bfloat16),
        preferred_element_type=jnp.float32,
    )
    rank = jnp.where(named, rank, -1.0)
    tail = jnp.where(third, rank, jnp.where(first, coarse.astype(jnp.float32), rest))
    mine = ring.block(0, ring.core)
    all_ref[mine, :, width - start :] = tail.astype(jnp.bfloat16)
    all_ref[mine, :, :width] = normed

    def last(index, j):
        return (j == 0) == (index == 0)

    def hop(index, way, step, j):
        view = all_ref.at[ring.block(-way * step, ring.core), chunks[j]]
        return remote(view, view, hop_send.at[index, step, j], hop_recv.at[index, step, j], ring.device(way))

    def relay(slot, offset, j):
        view = all_ref.at[ring.block(offset, ring.core), chunks[j]]
        return remote(view, view, copy_send.at[slot, j], copy_recv.at[slot, j], ring.partner)

    def forward(step, j):
        for index, way in ways:
            if isinstance(step, int) and step == half and not last(index, j):
                continue
            hop(index, way, step - 1, j).wait_recv()
            if last(index, j):
                if not (isinstance(step, int) and step == half):
                    hop(index, way, step, j).start()
            elif not isinstance(step, int):

                @pl.when(step < half - 1)
                def _():
                    hop(index, way, step, j).start()

            elif step < half - 1:
                hop(index, way, step, j).start()
            relay(index * half + step, -way * step, j).start()

    def share(slot, offset):
        return remote(
            term_ref.at[ring.block(offset, 1 - ring.core)], got.at[slot], pair_send.at[slot], pair_recv.at[slot], ring.partner
        )

    def compute(offsets, hooks):
        blocks = [ring.block(offset, core) for offset in offsets for core in range(CORES)]
        used = len(blocks) * capacity
        expert = ctx
        for i, block in enumerate(blocks):
            tail = all_ref[block, :, width - start :]
            lane = lax.broadcasted_iota(jnp.int32, (LANES, LANES), 1) - start
            line = lax.broadcasted_iota(jnp.int32, (LANES, LANES), 0)
            pick = ((line == 0) & ((lane == expert) | (lane == expert + experts))) | (
                (line == 1) & (lane == expert + 2 * experts)
            )
            across = lax.dot_general(
                pick.astype(jnp.float32).astype(jnp.bfloat16), tail, turned, preferred_element_type=jnp.float32
            )
            slot = lax.broadcasted_iota(jnp.int32, (capacity, rows), 0).astype(jnp.float32)
            match = across[1:2] == slot
            gate = jnp.sum(jnp.where(match, across[:1], 0.0), axis=1, keepdims=True)
            here = lax.broadcasted_iota(jnp.int32, (rows, LANES), 1) - start == expert + 2 * experts
            down_rank = jnp.sum(jnp.where(here, tail.astype(jnp.float32), 0.0), axis=1, keepdims=True)
            slot_down = lax.broadcasted_iota(jnp.int32, (rows, capacity), 1).astype(jnp.float32)
            span = slice(i * capacity, (i + 1) * capacity)
            picked = jnp.dot(
                match.astype(jnp.float32).astype(jnp.bfloat16), all_ref[block, :, :width], preferred_element_type=jnp.float32
            )
            rows_ref[span, :] = picked.astype(jnp.bfloat16)
            gate_ref[span, :] = gate
            back_ref[i] = (down_rank == slot_down).astype(jnp.float32).astype(jnp.bfloat16)

        def multiply(t, carry):
            span = pl.ds(pl.multiple_of(t * tile, 8), tile)
            x = rows_ref[:used, :]
            a = lax.dot_general(x, up_ref[0, span, :], turned, preferred_element_type=jnp.float32)
            b = lax.dot_general(x, up_ref[1, span, :], turned, preferred_element_type=jnp.float32)
            act_ref[t, :used, :] = (a * jax.nn.sigmoid(1.702 * a) * (b + 1.0)).astype(jnp.bfloat16)
            for spot, hook in enumerate(hooks):

                @pl.when(t == spot)
                def _():
                    hook()

            return carry

        lax.fori_loop(0, act_ref.shape[0], multiply, 0)
        for first in range(0, width, columns):
            span = slice(first, min(first + columns, width))
            piece = 0.0
            for t in range(act_ref.shape[0]):
                piece = piece + jnp.dot(
                    act_ref[t, :used, :], down_ref[t * tile : (t + 1) * tile, span], preferred_element_type=jnp.float32
                )
            gated = (piece * gate_ref[:used, :]).astype(jnp.bfloat16)
            for i, block in enumerate(blocks):
                term = jnp.dot(back_ref[i], gated[i * capacity : (i + 1) * capacity], preferred_element_type=jnp.float32)
                term_ref[block, :, span] = term.astype(jnp.bfloat16)

    for j in parts:
        for index, way in ways:
            if half > 1 or last(index, j):
                hop(index, way, 0, j).start()
        relay(0, 0, j).start()
    for copy in loads:
        copy.wait()
    for j in parts:
        relay(0, 0, j).wait_recv()
    compute([0], [])
    share(0, 0).start()
    for j in parts:
        forward(1, j)

    def ready(distance):
        for index, way in ways:
            for j in parts:
                relay(index * half + distance, -way * distance, j).wait_recv()

    def pair_up(distance):
        for index, way in ways:
            share(index * half + distance, -way * distance).start()

    def travel(distance, carry):
        ready(distance)
        compute(
            [-way * distance for index, way in ways], [functools.partial(forward, distance + 1, j) for j in parts]
        )
        pair_up(distance)
        return carry

    lax.fori_loop(1, half - 1, travel, 0)
    ready(half - 1)
    compute([1 - half, half - 1], [functools.partial(forward, half, j) for j in parts])
    pair_up(half - 1)
    for j in parts:
        for index, way in ways:
            if last(index, j):
                relay(index * half + half, -way * half, j).wait_recv()
    compute([half], [])
    share(half, half).start()

    arrived, hops = set(), {}

    def slot_of(offset):
        return offset + half if 0 < offset < half else abs(offset)

    def pair(offset, chunk):
        offset = half if offset == -half else offset
        if offset not in arrived:
            share(slot_of(offset), offset).wait_recv()
            arrived.add(offset)
        mine = term_ref[ring.block(offset, ring.core), chunk, :].astype(jnp.float32)
        return mine + got[slot_of(offset), chunk, :].astype(jnp.float32)

    for step in range(half):
        for j, chunk in enumerate(chunks):
            for index, way in ways:
                if step == 0 and not last(index, j):
                    continue
                total = pair(way * (half - step), chunk)
                if (index, step - 1, j) in hops:
                    hops[index, step - 1, j].wait_recv()
                    total = total + incoming[index, step - 1, chunk, :].astype(jnp.float32)
                outgoing[index, step, chunk, :] = total.astype(jnp.bfloat16)
                hops[index, step, j] = remote(
                    outgoing.at[index, step, chunk],
                    incoming.at[index, step, chunk],
                    ring_send.at[index, step, j],
                    ring_recv.at[index, step, j],
                    ring.device(way),
                )
                hops[index, step, j].start()
    for j, chunk in enumerate(chunks):
        total = pair(0, chunk) + residual_ref[chunk, :].astype(jnp.float32)
        for index in (0, 1):
            if (index, half - 1, j) in hops:
                hops[index, half - 1, j].wait_recv()
                total = total + incoming[index, half - 1, chunk, :].astype(jnp.float32)
        out_ref[chunk, :] = total.astype(jnp.bfloat16)

    for copy in sends + list(hops.values()):
        copy.wait_send()
    share(0, 0).wait_send()
    share(half, half).wait_send()
    for j in parts:
        relay(0, 0, j).wait_send()
        for index, way in ways:
            if last(index, j):
                hop(index, way, half - 1, j).wait_send()
                relay(index * half + half, -way * half, j).wait_send()
            hop(index, way, 0, j).wait_send()

    def drain(step, carry):
        for index, way in ways:
            share(index * half + step, -way * step).wait_send()
            for j in parts:
                relay(index * half + step, -way * step, j).wait_send()

                @pl.when(step < half - 1)
                def _():
                    hop(index, way, step, j).wait_send()

        return carry

    lax.fori_loop(1, half, drain, 0)


def norm_and_experts(partial_sums, hidden, norm_gain, router, routes, w_gate_up, w_down, capacity):
    chips, heads = lax.axis_size("ctx") // CORES, lax.axis_size("head")
    tokens, width = hidden.shape
    rows = tokens // heads
    experts = router.shape[1]
    hidden_units = w_down.shape[1]
    padded = width - width % LANES + LANES
    half = chips * heads // 2
    blocks = chips * heads * CORES
    parts = len(row_chunks(rows))
    capacity = -(-capacity // 16) * 16
    tile = hidden_units // 3 if hidden_units % 48 == 0 else hidden_units
    columns = 8 * LANES
    most = 2 * CORES
    bf16, f32, dma = jnp.bfloat16, jnp.float32, pltpu.SemaphoreType.DMA
    anywhere = pl.BlockSpec(memory_space=pl.ANY)
    return pl.pallas_call(
        functools.partial(layer_kernel, chips, heads, experts, capacity, tile, columns),
        out_shape=jax.ShapeDtypeStruct((rows, width), bf16),
        in_specs=[full_vmem()] * 5 + [anywhere] * 2,
        out_specs=full_vmem(),
        scratch_shapes=[
            pltpu.VMEM((blocks, rows, padded), bf16),
            pltpu.VMEM((rows, width), bf16),
            pltpu.VMEM((tokens, width), bf16),
            pltpu.VMEM((tokens, routes.shape[1]), f32),
            pltpu.VMEM((LANES, width), bf16),
            pltpu.VMEM((heads - 1, rows, width), bf16),
            pltpu.VMEM((2, hidden_units, width), bf16),
            pltpu.VMEM((hidden_units, width), bf16),
            pltpu.VMEM((most * capacity, width), bf16),
            pltpu.VMEM((hidden_units // tile, most * capacity, tile), bf16),
            pltpu.VMEM((most * capacity, 1), f32),
            pltpu.VMEM((most, rows, capacity), bf16),
            pltpu.VMEM((blocks, rows, width), bf16),
            pltpu.VMEM((2 * half, rows, width), bf16),
            pltpu.VMEM((2, half, rows, width), bf16),
            pltpu.VMEM((2, half, rows, width), bf16),
            dma((2,)),
            dma((heads - 1,)),
            dma((heads - 1,)),
            dma((2, half, parts)),
            dma((2, half, parts)),
            dma((2 * half + 1, parts)),
            dma((2 * half + 1, parts)),
            dma((2 * half,)),
            dma((2 * half,)),
            dma((2, half, parts)),
            dma((2, half, parts)),
        ],
        compiler_params=pltpu.CompilerParams(
            collective_id=1, has_side_effects=True, vmem_limit_bytes=60 * 1024 * 1024
        ),
        name="norm_and_experts",
    )(
        partial_sums,
        hidden.T,
        norm_gain.reshape(1, -1),
        router.T,
        routes.T,
        jnp.swapaxes(w_gate_up[0], 1, 2),
        w_down[0],
    )


def body(
    queries,
    keys,
    values,
    sinks,
    segments,
    hidden_in,
    routes,
    w_out,
    norm_gain,
    router,
    w_gate_up,
    w_down,
):
    n_ctx = lax.axis_size("ctx")
    n_head = lax.axis_size("head")
    tok_count = queries.shape[0]
    top_count = routes.shape[1]
    q_start = lax.axis_index("ctx") * tok_count
    tok_pos = q_start + jnp.arange(tok_count, dtype=jnp.int32)
    tok_seg = lax.dynamic_slice_in_dim(segments, q_start, tok_count, 0)
    all_keys, all_values = gather_keys(keys, values)
    attended = attend(queries, all_keys, all_values, sinks, tok_pos, tok_seg, segments)
    capacity = max(2, min(tok_count // n_head, 3 * tok_count * top_count // (2 * n_head * n_ctx)))
    partial_sums = jnp.dot(attended, w_out, preferred_element_type=jnp.float32).astype(jnp.bfloat16)
    return norm_and_experts(partial_sums, hidden_in, norm_gain, router, routes, w_gate_up, w_down, capacity)


def solution(mesh):
    placed = (
        P(("group", "ctx"), "head"),
        P(("group", "ctx"), "head"),
        P(("group", "ctx"), "head"),
        P("head"),
        P("group"),
        P(("group", "ctx"), None),
        P(("group", "ctx"), None),
        P("head", None),
        P(),
        P(),
        P("ctx", None, None, "head"),
        P("ctx", "head", None),
    )
    return jax.shard_map(
        body,
        mesh=mesh,
        in_specs=placed,
        out_specs=P(("group", "ctx", "head"), None),
        check_vma=False,
    )
```

```python
import functools
import math

import jax
import jax.numpy as jnp
from jax import lax
from jax.experimental import pallas as pl
from jax.experimental.pallas import tpu as pltpu
from jax.sharding import PartitionSpec as P

HEAD_SIZE = 64


masked_value = -1e30


MESH = pl.DeviceIdType.MESH
LANES = 128
CORES = 2


def full_vmem():
    return pl.BlockSpec(memory_space=pltpu.VMEM)


class Ring:
    def __init__(self, chips, heads):
        self.chips, self.heads, self.count = chips, heads, chips * heads
        ctx = lax.axis_index("ctx")
        self.head = lax.axis_index("head")
        self.core = lax.rem(ctx, CORES)
        z = lax.div(ctx, CORES)
        self.place = self.head * chips + z + lax.rem(self.head, 2) * (chips - 1 - 2 * z)
        self.partner = {"ctx": z * CORES + 1 - self.core, "head": self.head}

    def at(self, offset):
        spot = lax.rem(self.place + offset + self.count, self.count)
        head = lax.div(spot, self.chips)
        step = lax.rem(spot, self.chips)
        return head, step + lax.rem(head, 2) * (self.chips - 1 - 2 * step)

    def block(self, offset, core):
        head, z = self.at(offset)
        return (z * CORES + core) * self.heads + head

    def device(self, offset):
        head, z = self.at(offset)
        return {"ctx": z * CORES + self.core, "head": head}


def remote(src, dst, send_sem, recv_sem, device):
    return pltpu.make_async_remote_copy(
        src_ref=src, dst_ref=dst, send_sem=send_sem, recv_sem=recv_sem, device_id=device, device_id_type=MESH
    )


def row_chunks(rows):
    if rows % 32 == 0:
        return [pl.ds(0, rows // 2), pl.ds(rows // 2, rows // 2)]
    return [pl.ds(0, rows)]


def attend_kernel(
    chips, heads, key_ref, value_ref, query_ref, sink_ref, segment_ref, hidden_ref, weight_hbm, out_ref,
    all_keys, all_values, stacked, group_keys, group_values, bias_ref, score_ref, peak_ref, attended_ref, weight_ref,
    hidden_rows, part_ref, slots,
    line_send, line_recv, pair_send, pair_recv, head_send, head_recv, weight_sem,
):
    ctx, head = lax.axis_index("ctx"), lax.axis_index("head")
    z, core = lax.div(ctx, CORES), lax.rem(ctx, CORES)
    rows = query_ref.shape[0]
    groups = key_ref.shape[1] // HEAD_SIZE
    share = query_ref.shape[1] // key_ref.shape[1]
    keys = CORES * rows
    own_rows, width = out_ref.shape
    ins, alls = (key_ref, value_ref), (all_keys, all_values)
    turned = (((1,), (1,)), ((), ()))
    partner = {"ctx": z * CORES + 1 - core}
    above = {"ctx": (z + 1) * CORES + core}
    others = [{"ctx": ctx, "head": lax.rem(head + turn, heads)} for turn in range(1, heads)]
    has_above, has_below = z + 1 < chips, z > 0
    load = pltpu.make_async_copy(weight_hbm, weight_ref, weight_sem)
    load.start()

    barrier = pltpu.get_barrier_semaphore()
    for device in [partner] + others:
        pl.semaphore_signal(barrier, inc=1, device_id=device, device_id_type=MESH)

    @pl.when(has_above)
    def _():
        pl.semaphore_signal(barrier, inc=1, device_id=above, device_id_type=MESH)

    @pl.when(has_below)
    def _():
        pl.semaphore_signal(barrier, inc=1, device_id={"ctx": (z - 1) * CORES + core}, device_id_type=MESH)

    peers = heads + jnp.where(has_above, 1, 0) + jnp.where(has_below, 1, 0)
    pl.semaphore_wait(barrier, peers)

    def hop(step, part):
        block = (z - step) * CORES + core
        source = ins[part] if step == 0 else alls[part].at[block]
        return remote(source, alls[part].at[block], line_send.at[step, part], line_recv.at[step, part], above)

    def relay(step, part):
        block = (z - step) * CORES + core
        source = ins[part] if step == 0 else alls[part].at[block]
        return remote(source, alls[part].at[block], pair_send.at[step, part], pair_recv.at[step, part], partner)

    for part in (0, 1):

        @pl.when(has_above)
        def _():
            hop(0, part).start()

        relay(0, part).start()
    for part in (0, 1):
        alls[part][ctx] = ins[part][...]

    for index in range(groups * share):
        span = slice(index * HEAD_SIZE, (index + 1) * HEAD_SIZE)
        stacked[index // share, index % share * rows : (index % share + 1) * rows, :] = query_ref[:, span]
    lane = lax.broadcasted_iota(jnp.int32, group_values.shape[1:], 1)
    for group in range(groups):
        group_values[group] = (lane == HEAD_SIZE).astype(jnp.float32).astype(jnp.bfloat16)
    here = pl.ds(pl.multiple_of(ctx * rows, rows), rows)
    diagonal = lax.broadcasted_iota(jnp.int32, (rows, rows), 0) == lax.broadcasted_iota(jnp.int32, (rows, rows), 1)
    own_segment = jnp.sum(
        jnp.where(diagonal, segment_ref[:, here].astype(jnp.float32), 0.0), axis=1, keepdims=True
    )
    log2e = math.log2(math.e)
    factor = HEAD_SIZE ** (-0.5) * log2e

    def score(step):
        chip = z - step
        block = all_keys[pl.ds(chip * CORES, CORES)].reshape(keys, key_ref.shape[1])
        for group in range(groups):
            group_keys[group] = block[:, group * HEAD_SIZE : (group + 1) * HEAD_SIZE]
        spot = lax.broadcasted_iota(jnp.int32, (rows, keys), 1) + chip * keys
        place = lax.broadcasted_iota(jnp.int32, (rows, keys), 0) + ctx * rows
        segment = segment_ref[:, pl.ds(pl.multiple_of(chip * keys, keys), keys)].astype(jnp.float32)
        bias_ref[...] = jnp.where((spot <= place) & (segment == own_segment), 0.0, masked_value)

        def one(group, carry):
            scores = lax.dot_general(stacked[group], group_keys[group], turned, preferred_element_type=jnp.float32)
            scores = scores.reshape(share, rows, keys) * factor + bias_ref[...]
            span = pl.ds(group * share, share)
            score_ref[step, span] = scores
            peak = scores[:, :, :LANES]
            for first in range(LANES, keys, LANES):
                peak = jnp.maximum(peak, scores[:, :, first : first + LANES])
            peak_ref[span] = peak if step == 0 else jnp.maximum(peak_ref[span], peak)
            return carry

        lax.fori_loop(0, groups, one, 0)

    def take_values(step):
        relay(step, 1).wait_recv()
        block = all_values[pl.ds((z - step) * CORES, CORES)].reshape(keys, value_ref.shape[1])
        for group in range(groups):
            group_values[group, step * keys : (step + 1) * keys, :HEAD_SIZE] = block[
                :, group * HEAD_SIZE : (group + 1) * HEAD_SIZE
            ]

    relay(0, 0).wait_recv()
    score(0)
    for step in range(1, chips):

        @pl.when(z - step >= 0)
        def _():
            for part in (0, 1):
                hop(step - 1, part).wait_recv()
                if step < chips - 1:

                    @pl.when(has_above)
                    def _():
                        hop(step, part).start()

                relay(step, part).start()
            take_values(step - 1)
            relay(step, 0).wait_recv()
            score(step)

        @pl.when(z - step < 0)
        def _():
            @pl.when(z - step == -1)
            def _():
                take_values(step - 1)

            def blank(index, carry):
                score_ref[step, index] = jnp.full((rows, keys), masked_value, jnp.float32)
                return carry

            lax.fori_loop(0, groups * share, blank, 0)

    @pl.when(z == chips - 1)
    def _():
        take_values(chips - 1)

    own = pl.ds(pl.multiple_of(head * own_rows, own_rows), own_rows)
    hidden_rows[...] = hidden_ref[...].T

    def mix(couple, carry):
        group = lax.div(couple * 2, share)
        sinks, tops = [], []
        for member in range(2):
            sinks.append(sink_ref[couple * 2 + member] * log2e)
            peak = jnp.max(peak_ref[couple * 2 + member], axis=-1, keepdims=True)
            tops.append(jnp.maximum(peak, sinks[member]))
        mixed = jnp.zeros((2 * rows, LANES), jnp.float32)
        for step in range(chips):
            weights = jnp.concatenate(
                [
                    jnp.exp2(score_ref[step, couple * 2 + member] - tops[member]).astype(jnp.bfloat16)
                    for member in range(2)
                ],
                axis=0,
            )
            mixed = mixed + jnp.dot(
                weights, group_values[group, step * keys : (step + 1) * keys, :], preferred_element_type=jnp.float32
            )
        both = []
        for member in range(2):
            mine = mixed[member * rows : (member + 1) * rows]
            total = mine[:, HEAD_SIZE : HEAD_SIZE + 1] + jnp.exp2(sinks[member] - tops[member])
            both.append((mine[:, :HEAD_SIZE] / total).astype(jnp.bfloat16))
        span = pl.ds(pl.multiple_of(couple * 2 * HEAD_SIZE, 2 * HEAD_SIZE), 2 * HEAD_SIZE)
        attended_ref[:, span] = jnp.concatenate(both, axis=1)
        return carry

    lax.fori_loop(0, groups * share // 2, mix, 0)

    load.wait()
    spans = column_spans(part_ref.shape[1])
    part_ref[:, spans[-1][0] :] = jnp.zeros((rows, spans[-1][1]), part_ref.dtype)
    sends = {}
    for c, (first, size) in enumerate(spans):
        last = min(first + size, width)
        piece = lax.dot_general(
            attended_ref[...], weight_ref[first:last, :], turned, preferred_element_type=jnp.float32
        )
        part_ref[:, first:last] = piece.astype(jnp.bfloat16)
        for turn, device in enumerate(others):
            target = pl.ds(pl.multiple_of(device["head"] * own_rows, own_rows), own_rows)
            sends[turn, c] = remote(
                part_ref.at[target, pl.ds(first, size)],
                slots.at[turn, :, pl.ds(first, size)],
                head_send.at[turn, c],
                head_recv.at[turn, c],
                device,
            )
            sends[turn, c].start()
    for c, (first, size) in enumerate(spans):
        span = slice(first, min(first + size, width))
        total = hidden_rows[own, span].astype(jnp.float32) + part_ref[own, span].astype(jnp.float32)
        for turn in range(heads - 1):
            sends[turn, c].wait_recv()
            total = total + slots[turn, :, span].astype(jnp.float32)
        out_ref[:, span] = total.astype(jnp.bfloat16)

    for copy in sends.values():
        copy.wait_send()
    for part in (0, 1):
        for step in range(chips):

            @pl.when(z - step >= 0)
            def _():
                relay(step, part).wait_send()
                if step < chips - 1:

                    @pl.when(has_above)
                    def _():
                        hop(step, part).wait_send()


def column_spans(padded):
    wide = 8 * LANES
    return [(first, min(wide, padded - first)) for first in range(0, padded, wide)]


def attend(queries, keys, values, sinks, segments, hidden, w_out):
    chips, heads = lax.axis_size("ctx") // CORES, lax.axis_size("head")
    n_ctx = lax.axis_size("ctx")
    rows = queries.shape[0]
    width = w_out.shape[1]
    padded = -(-width // LANES) * LANES
    groups = keys.shape[1] // HEAD_SIZE
    share = queries.shape[1] // keys.shape[1]
    parts = len(column_spans(padded))
    bf16, f32, dma = jnp.bfloat16, jnp.float32, pltpu.SemaphoreType.DMA
    chip_keys = CORES * rows
    return pl.pallas_call(
        functools.partial(attend_kernel, chips, heads),
        out_shape=jax.ShapeDtypeStruct((rows // heads, width), bf16),
        in_specs=[full_vmem()] * 3
        + [pl.BlockSpec(memory_space=pltpu.SMEM)]
        + [full_vmem()] * 2
        + [pl.BlockSpec(memory_space=pl.ANY)],
        out_specs=full_vmem(),
        scratch_shapes=[
            pltpu.VMEM((n_ctx,) + keys.shape, bf16),
            pltpu.VMEM((n_ctx,) + keys.shape, bf16),
            pltpu.VMEM((groups, share * rows, HEAD_SIZE), bf16),
            pltpu.VMEM((groups, chip_keys, HEAD_SIZE), bf16),
            pltpu.VMEM((groups, chips * chip_keys, LANES), bf16),
            pltpu.VMEM((rows, chip_keys), f32),
            pltpu.VMEM((chips, groups * share, rows, chip_keys), f32),
            pltpu.VMEM((groups * share, rows, LANES), f32),
            pltpu.VMEM(queries.shape, bf16),
            pltpu.VMEM((width, w_out.shape[0]), bf16),
            pltpu.VMEM((rows, width), bf16),
            pltpu.VMEM((rows, padded), bf16),
            pltpu.VMEM((heads - 1, rows // heads, padded), bf16),
            dma((chips, 2)),
            dma((chips, 2)),
            dma((chips, 2)),
            dma((chips, 2)),
            dma((heads - 1, parts)),
            dma((heads - 1, parts)),
            dma(()),
        ],
        compiler_params=pltpu.CompilerParams(
            collective_id=0, has_side_effects=True, vmem_limit_bytes=60 * 1024 * 1024
        ),
        name="attend",
    )(keys, values, queries, sinks, segments.reshape(1, -1), hidden.T, w_out.T)


def layer_kernel(
    chips, heads, experts, capacity, tile, columns, residual_ref, gain_ref, router_ref, route_ref, up_hbm, down_hbm,
    out_ref, all_ref, route_rows, lanes_ref, up_ref, down_ref, rows_ref, act_ref,
    gate_ref, back_ref, term_ref, got, outgoing, incoming, weight_sem,
    hop_send, hop_recv, copy_send, copy_recv, pair_send, pair_recv, ring_send, ring_recv,
):
    ring = Ring(chips, heads)
    count, half = ring.count, ring.count // 2
    rows, width = out_ref.shape
    start = width % LANES
    chunks = row_chunks(rows)
    parts = range(len(chunks))
    ways = ((0, 1), (1, -1))
    turned = (((1,), (1,)), ((), ()))
    ctx, head = lax.axis_index("ctx"), ring.head

    barrier = pltpu.get_barrier_semaphore()
    peers = [ring.device(1), ring.device(-1), ring.partner]
    for device in peers:
        pl.semaphore_signal(barrier, inc=1, device_id=device, device_id_type=MESH)
    loads = [
        pltpu.make_async_copy(up_hbm, up_ref, weight_sem.at[0]),
        pltpu.make_async_copy(down_hbm, down_ref, weight_sem.at[1]),
    ]
    for copy in loads:
        copy.start()

    own = pl.ds(pl.multiple_of(head * rows, rows), rows)
    tokens = route_ref.shape[1]
    eye = (
        lax.broadcasted_iota(jnp.int32, (tokens, tokens), 0) == lax.broadcasted_iota(jnp.int32, (tokens, tokens), 1)
    ).astype(jnp.float32)
    route_rows[...] = lax.dot_general(
        eye.astype(jnp.bfloat16),
        route_ref[...].astype(jnp.float32).astype(jnp.bfloat16),
        turned,
        preferred_element_type=jnp.float32,
    )
    lanes_ref[...] = jnp.zeros(lanes_ref.shape, lanes_ref.dtype)
    lanes_ref[start : start + experts, :] = router_ref[...]
    lanes_ref[start + experts : start + 2 * experts, :] = router_ref[...]

    residual = residual_ref[...]
    wide = residual.astype(jnp.float32)
    scale = lax.rsqrt(jnp.mean(wide * wide, axis=-1, keepdims=True) + 1e-05)
    normed = (wide * scale * gain_ref[...]).astype(jnp.bfloat16)

    logits = lax.dot_general(normed, lanes_ref[...], turned, preferred_element_type=jnp.float32)
    lane = lax.broadcasted_iota(jnp.int32, logits.shape, 1) - start
    first = (lane >= 0) & (lane < experts)
    third = (lane >= 2 * experts) & (lane < 3 * experts)
    names = route_rows[own, :]
    present = jnp.zeros(logits.shape, jnp.bool_)
    named = jnp.zeros(logits.shape, jnp.bool_)
    spot = lane.astype(jnp.float32)
    for k in range(route_ref.shape[0]):
        name = names[:, k : k + 1]
        present = present | (spot == name) | (spot - experts == name)
        named = named | (spot - 2 * experts == name)
    top = jnp.max(jnp.where(present, logits, -jnp.inf), axis=-1, keepdims=True)
    powers = jnp.where(present, jnp.exp(jnp.where(present, logits - top, 0.0)), 0.0)
    gates = powers / jnp.sum(jnp.where(first, powers, 0.0), axis=-1, keepdims=True)
    coarse = gates.astype(jnp.bfloat16)
    rest = gates - coarse.astype(jnp.float32)
    earlier = lax.broadcasted_iota(jnp.int32, (rows, rows), 0) > lax.broadcasted_iota(jnp.int32, (rows, rows), 1)
    rank = jnp.dot(
        earlier.astype(jnp.float32).astype(jnp.bfloat16),
        named.astype(jnp.float32).astype(jnp.bfloat16),
        preferred_element_type=jnp.float32,
    )
    rank = jnp.where(named, rank, -1.0)
    tail = jnp.where(third, rank, jnp.where(first, coarse.astype(jnp.float32), rest))
    mine = ring.block(0, ring.core)
    all_ref[mine, :, width - start :] = tail.astype(jnp.bfloat16)
    all_ref[mine, :, :width] = normed

    def last(index, j):
        return (j == 0) == (index == 0)

    def hop(index, way, step, j):
        view = all_ref.at[ring.block(-way * step, ring.core), chunks[j]]
        return remote(view, view, hop_send.at[index, step, j], hop_recv.at[index, step, j], ring.device(way))

    def relay(slot, offset, j):
        view = all_ref.at[ring.block(offset, ring.core), chunks[j]]
        return remote(view, view, copy_send.at[slot, j], copy_recv.at[slot, j], ring.partner)

    def forward(step, j):
        for index, way in ways:
            if isinstance(step, int) and step == half and not last(index, j):
                continue
            hop(index, way, step - 1, j).wait_recv()
            if last(index, j):
                if not (isinstance(step, int) and step == half):
                    hop(index, way, step, j).start()
            elif not isinstance(step, int):

                @pl.when(step < half - 1)
                def _():
                    hop(index, way, step, j).start()

            elif step < half - 1:
                hop(index, way, step, j).start()
            relay(index * half + step, -way * step, j).start()

    def share(slot, offset):
        return remote(
            term_ref.at[ring.block(offset, 1 - ring.core)], got.at[slot], pair_send.at[slot], pair_recv.at[slot], ring.partner
        )

    def compute(offsets, hooks):
        blocks = [ring.block(offset, core) for offset in offsets for core in range(CORES)]
        used = len(blocks) * capacity
        expert = ctx
        for i, block in enumerate(blocks):
            tail = all_ref[block, :, width - start :]
            lane = lax.broadcasted_iota(jnp.int32, (LANES, LANES), 1) - start
            line = lax.broadcasted_iota(jnp.int32, (LANES, LANES), 0)
            pick = ((line == 0) & ((lane == expert) | (lane == expert + experts))) | (
                (line == 1) & (lane == expert + 2 * experts)
            )
            across = lax.dot_general(
                pick.astype(jnp.float32).astype(jnp.bfloat16), tail, turned, preferred_element_type=jnp.float32
            )
            slot = lax.broadcasted_iota(jnp.int32, (capacity, rows), 0).astype(jnp.float32)
            match = across[1:2] == slot
            gate = jnp.sum(jnp.where(match, across[:1], 0.0), axis=1, keepdims=True)
            here = lax.broadcasted_iota(jnp.int32, (rows, LANES), 1) - start == expert + 2 * experts
            down_rank = jnp.sum(jnp.where(here, tail.astype(jnp.float32), 0.0), axis=1, keepdims=True)
            slot_down = lax.broadcasted_iota(jnp.int32, (rows, capacity), 1).astype(jnp.float32)
            span = slice(i * capacity, (i + 1) * capacity)
            picked = jnp.dot(
                match.astype(jnp.float32).astype(jnp.bfloat16), all_ref[block, :, :width], preferred_element_type=jnp.float32
            )
            rows_ref[span, :] = picked.astype(jnp.bfloat16)
            gate_ref[span, :] = gate
            back_ref[i] = (down_rank == slot_down).astype(jnp.float32).astype(jnp.bfloat16)

        def multiply(t, carry):
            span = pl.ds(pl.multiple_of(t * tile, 8), tile)
            x = rows_ref[:used, :]
            a = lax.dot_general(x, up_ref[0, span, :], turned, preferred_element_type=jnp.float32)
            b = lax.dot_general(x, up_ref[1, span, :], turned, preferred_element_type=jnp.float32)
            act_ref[t, :used, :] = (a * jax.nn.sigmoid(1.702 * a) * (b + 1.0)).astype(jnp.bfloat16)
            for spot, hook in enumerate(hooks):

                @pl.when(t == spot)
                def _():
                    hook()

            return carry

        lax.fori_loop(0, act_ref.shape[0], multiply, 0)
        for first in range(0, width, columns):
            span = slice(first, min(first + columns, width))
            piece = 0.0
            for t in range(act_ref.shape[0]):
                piece = piece + jnp.dot(
                    act_ref[t, :used, :], down_ref[t * tile : (t + 1) * tile, span], preferred_element_type=jnp.float32
                )
            gated = (piece * gate_ref[:used, :]).astype(jnp.bfloat16)
            for i, block in enumerate(blocks):
                term = jnp.dot(back_ref[i], gated[i * capacity : (i + 1) * capacity], preferred_element_type=jnp.float32)
                term_ref[block, :, span] = term.astype(jnp.bfloat16)

    pl.semaphore_wait(barrier, len(peers))
    for j in parts:
        for index, way in ways:
            if half > 1 or last(index, j):
                hop(index, way, 0, j).start()
        relay(0, 0, j).start()
    for copy in loads:
        copy.wait()
    for j in parts:
        relay(0, 0, j).wait_recv()
    compute([0], [])
    share(0, 0).start()
    for j in parts:
        forward(1, j)

    def ready(distance):
        for index, way in ways:
            for j in parts:
                relay(index * half + distance, -way * distance, j).wait_recv()

    def pair_up(distance):
        for index, way in ways:
            share(index * half + distance, -way * distance).start()

    def travel(distance, carry):
        ready(distance)
        compute(
            [-way * distance for index, way in ways], [functools.partial(forward, distance + 1, j) for j in parts]
        )
        pair_up(distance)
        return carry

    lax.fori_loop(1, half - 1, travel, 0)
    ready(half - 1)
    compute([1 - half, half - 1], [functools.partial(forward, half, j) for j in parts])
    pair_up(half - 1)
    for j in parts:
        for index, way in ways:
            if last(index, j):
                relay(index * half + half, -way * half, j).wait_recv()
    compute([half], [])
    share(half, half).start()

    arrived, hops = set(), {}

    def slot_of(offset):
        return offset + half if 0 < offset < half else abs(offset)

    def pair(offset, chunk):
        offset = half if offset == -half else offset
        if offset not in arrived:
            share(slot_of(offset), offset).wait_recv()
            arrived.add(offset)
        mine = term_ref[ring.block(offset, ring.core), chunk, :].astype(jnp.float32)
        return mine + got[slot_of(offset), chunk, :].astype(jnp.float32)

    for step in range(half):
        for j, chunk in enumerate(chunks):
            for index, way in ways:
                if step == 0 and not last(index, j):
                    continue
                total = pair(way * (half - step), chunk)
                if (index, step - 1, j) in hops:
                    hops[index, step - 1, j].wait_recv()
                    total = total + incoming[index, step - 1, chunk, :].astype(jnp.float32)
                outgoing[index, step, chunk, :] = total.astype(jnp.bfloat16)
                hops[index, step, j] = remote(
                    outgoing.at[index, step, chunk],
                    incoming.at[index, step, chunk],
                    ring_send.at[index, step, j],
                    ring_recv.at[index, step, j],
                    ring.device(way),
                )
                hops[index, step, j].start()
    for j, chunk in enumerate(chunks):
        total = pair(0, chunk) + residual_ref[chunk, :].astype(jnp.float32)
        for index in (0, 1):
            if (index, half - 1, j) in hops:
                hops[index, half - 1, j].wait_recv()
                total = total + incoming[index, half - 1, chunk, :].astype(jnp.float32)
        out_ref[chunk, :] = total.astype(jnp.bfloat16)

    for copy in hops.values():
        copy.wait_send()
    share(0, 0).wait_send()
    share(half, half).wait_send()
    for j in parts:
        relay(0, 0, j).wait_send()
        for index, way in ways:
            if last(index, j):
                hop(index, way, half - 1, j).wait_send()
                relay(index * half + half, -way * half, j).wait_send()
            hop(index, way, 0, j).wait_send()

    def drain(step, carry):
        for index, way in ways:
            share(index * half + step, -way * step).wait_send()
            for j in parts:
                relay(index * half + step, -way * step, j).wait_send()

                @pl.when(step < half - 1)
                def _():
                    hop(index, way, step, j).wait_send()

        return carry

    lax.fori_loop(1, half, drain, 0)


def norm_and_experts(residual, norm_gain, router, routes, w_gate_up, w_down, capacity):
    chips, heads = lax.axis_size("ctx") // CORES, lax.axis_size("head")
    rows, width = residual.shape
    tokens = rows * heads
    experts = router.shape[1]
    hidden_units = w_down.shape[1]
    padded = width - width % LANES + LANES
    half = chips * heads // 2
    blocks = chips * heads * CORES
    parts = len(row_chunks(rows))
    capacity = -(-capacity // 16) * 16
    tile = hidden_units // 3 if hidden_units % 48 == 0 else hidden_units
    columns = 8 * LANES
    most = 2 * CORES
    bf16, f32, dma = jnp.bfloat16, jnp.float32, pltpu.SemaphoreType.DMA
    anywhere = pl.BlockSpec(memory_space=pl.ANY)
    return pl.pallas_call(
        functools.partial(layer_kernel, chips, heads, experts, capacity, tile, columns),
        out_shape=jax.ShapeDtypeStruct((rows, width), bf16),
        in_specs=[full_vmem()] * 4 + [anywhere] * 2,
        out_specs=full_vmem(),
        scratch_shapes=[
            pltpu.VMEM((blocks, rows, padded), bf16),
            pltpu.VMEM((tokens, routes.shape[1]), f32),
            pltpu.VMEM((LANES, width), bf16),
            pltpu.VMEM((2, hidden_units, width), bf16),
            pltpu.VMEM((hidden_units, width), bf16),
            pltpu.VMEM((most * capacity, width), bf16),
            pltpu.VMEM((hidden_units // tile, most * capacity, tile), bf16),
            pltpu.VMEM((most * capacity, 1), f32),
            pltpu.VMEM((most, rows, capacity), bf16),
            pltpu.VMEM((blocks, rows, width), bf16),
            pltpu.VMEM((2 * half, rows, width), bf16),
            pltpu.VMEM((2, half, rows, width), bf16),
            pltpu.VMEM((2, half, rows, width), bf16),
            dma((2,)),
            dma((2, half, parts)),
            dma((2, half, parts)),
            dma((2 * half + 1, parts)),
            dma((2 * half + 1, parts)),
            dma((2 * half,)),
            dma((2 * half,)),
            dma((2, half, parts)),
            dma((2, half, parts)),
        ],
        compiler_params=pltpu.CompilerParams(
            collective_id=1, has_side_effects=True, vmem_limit_bytes=60 * 1024 * 1024
        ),
        name="norm_and_experts",
    )(
        residual,
        norm_gain.reshape(1, -1),
        router.T,
        routes.T,
        jnp.swapaxes(w_gate_up[0], 1, 2),
        w_down[0],
    )


def body(
    queries,
    keys,
    values,
    sinks,
    segments,
    hidden_in,
    routes,
    w_out,
    norm_gain,
    router,
    w_gate_up,
    w_down,
):
    n_ctx = lax.axis_size("ctx")
    n_head = lax.axis_size("head")
    tok_count = queries.shape[0]
    top_count = routes.shape[1]
    capacity = max(2, min(tok_count // n_head, 3 * tok_count * top_count // (2 * n_head * n_ctx)))
    residual = attend(queries, keys, values, sinks, segments, hidden_in, w_out)
    return norm_and_experts(residual, norm_gain, router, routes, w_gate_up, w_down, capacity)


def solution(mesh):
    placed = (
        P(("group", "ctx"), "head"),
        P(("group", "ctx"), "head"),
        P(("group", "ctx"), "head"),
        P("head"),
        P("group"),
        P(("group", "ctx"), None),
        P(("group", "ctx"), None),
        P("head", None),
        P(),
        P(),
        P("ctx", None, None, "head"),
        P("ctx", "head", None),
    )
    return jax.shard_map(
        body,
        mesh=mesh,
        in_specs=placed,
        out_specs=P(("group", "ctx", "head"), None),
        check_vma=False,
    )
```

```python
import functools
import math

import jax
import jax.numpy as jnp
from jax import lax
from jax.experimental import pallas as pl
from jax.experimental.pallas import tpu as pltpu
from jax.sharding import PartitionSpec as P

HEAD_SIZE = 64


masked_value = -1e30


MESH = pl.DeviceIdType.MESH
LANES = 128
CORES = 2


def full_vmem():
    return pl.BlockSpec(memory_space=pltpu.VMEM)


class Ring:
    def __init__(self, chips, heads):
        self.chips, self.heads, self.count = chips, heads, chips * heads
        ctx = lax.axis_index("ctx")
        self.head = lax.axis_index("head")
        self.core = lax.rem(ctx, CORES)
        z = lax.div(ctx, CORES)
        self.place = self.head * chips + z + lax.rem(self.head, 2) * (chips - 1 - 2 * z)
        self.partner = {"ctx": z * CORES + 1 - self.core, "head": self.head}

    def at(self, offset):
        spot = lax.rem(self.place + offset + self.count, self.count)
        head = lax.div(spot, self.chips)
        step = lax.rem(spot, self.chips)
        return head, step + lax.rem(head, 2) * (self.chips - 1 - 2 * step)

    def block(self, offset, core):
        head, z = self.at(offset)
        return (z * CORES + core) * self.heads + head

    def device(self, offset):
        head, z = self.at(offset)
        return {"ctx": z * CORES + self.core, "head": head}


def remote(src, dst, send_sem, recv_sem, device):
    return pltpu.make_async_remote_copy(
        src_ref=src, dst_ref=dst, send_sem=send_sem, recv_sem=recv_sem, device_id=device, device_id_type=MESH
    )


def row_chunks(rows):
    if rows % 32 == 0:
        return [pl.ds(0, rows // 2), pl.ds(rows // 2, rows // 2)]
    return [pl.ds(0, rows)]


def attend_kernel(
    chips, heads, key_ref, value_ref, query_ref, sink_ref, segment_ref, hidden_ref, weight_hbm, out_ref,
    all_keys, all_values, stacked, group_keys, group_values, bias_ref, score_ref, peak_ref, attended_ref, weight_ref,
    hidden_rows, part_ref, slots,
    line_send, line_recv, pair_send, pair_recv, head_send, head_recv, weight_sem,
):
    ctx, head = lax.axis_index("ctx"), lax.axis_index("head")
    z, core = lax.div(ctx, CORES), lax.rem(ctx, CORES)
    rows = query_ref.shape[0]
    groups = key_ref.shape[1] // HEAD_SIZE
    share = query_ref.shape[1] // key_ref.shape[1]
    keys = CORES * rows
    own_rows, width = out_ref.shape
    ins, alls = (key_ref, value_ref), (all_keys, all_values)
    turned = (((1,), (1,)), ((), ()))
    partner = {"ctx": z * CORES + 1 - core}
    above = {"ctx": (z + 1) * CORES + core}
    others = [{"ctx": ctx, "head": lax.rem(head + turn, heads)} for turn in range(1, heads)]
    has_above, has_below = z + 1 < chips, z > 0
    load = pltpu.make_async_copy(weight_hbm, weight_ref, weight_sem)
    load.start()

    barrier = pltpu.get_barrier_semaphore()
    for device in [partner] + others:
        pl.semaphore_signal(barrier, inc=1, device_id=device, device_id_type=MESH)

    @pl.when(has_above)
    def _():
        pl.semaphore_signal(barrier, inc=1, device_id=above, device_id_type=MESH)

    @pl.when(has_below)
    def _():
        pl.semaphore_signal(barrier, inc=1, device_id={"ctx": (z - 1) * CORES + core}, device_id_type=MESH)

    peers = heads + jnp.where(has_above, 1, 0) + jnp.where(has_below, 1, 0)
    pl.semaphore_wait(barrier, peers)

    def hop(step, part):
        block = (z - step) * CORES + core
        source = ins[part] if step == 0 else alls[part].at[block]
        return remote(source, alls[part].at[block], line_send.at[step, part], line_recv.at[step, part], above)

    def relay(step, part):
        block = (z - step) * CORES + core
        source = ins[part] if step == 0 else alls[part].at[block]
        return remote(source, alls[part].at[block], pair_send.at[step, part], pair_recv.at[step, part], partner)

    for part in (0, 1):

        @pl.when(has_above)
        def _():
            hop(0, part).start()

        relay(0, part).start()
    for part in (0, 1):
        alls[part][ctx] = ins[part][...]

    for index in range(groups * share):
        span = slice(index * HEAD_SIZE, (index + 1) * HEAD_SIZE)
        stacked[index // share, index % share * rows : (index % share + 1) * rows, :] = query_ref[:, span]
    lane = lax.broadcasted_iota(jnp.int32, group_values.shape[1:], 1)
    for group in range(groups):
        group_values[group] = (lane == HEAD_SIZE).astype(jnp.float32).astype(jnp.bfloat16)
    here = pl.ds(pl.multiple_of(ctx * rows, rows), rows)
    diagonal = lax.broadcasted_iota(jnp.int32, (rows, rows), 0) == lax.broadcasted_iota(jnp.int32, (rows, rows), 1)
    own_segment = jnp.sum(
        jnp.where(diagonal, segment_ref[:, here].astype(jnp.float32), 0.0), axis=1, keepdims=True
    )
    log2e = math.log2(math.e)
    factor = HEAD_SIZE ** (-0.5) * log2e

    def score(step):
        chip = z - step
        block = all_keys[pl.ds(chip * CORES, CORES)].reshape(keys, key_ref.shape[1])
        for group in range(groups):
            group_keys[group] = block[:, group * HEAD_SIZE : (group + 1) * HEAD_SIZE]
        spot = lax.broadcasted_iota(jnp.int32, (rows, keys), 1) + chip * keys
        place = lax.broadcasted_iota(jnp.int32, (rows, keys), 0) + ctx * rows
        segment = segment_ref[:, pl.ds(pl.multiple_of(chip * keys, keys), keys)].astype(jnp.float32)
        bias_ref[...] = jnp.where((spot <= place) & (segment == own_segment), 0.0, masked_value)

        def one(group, carry):
            scores = lax.dot_general(stacked[group], group_keys[group], turned, preferred_element_type=jnp.float32)
            scores = scores.reshape(share, rows, keys) * factor + bias_ref[...]
            span = pl.ds(group * share, share)
            score_ref[step, span] = scores
            peak = scores[:, :, :LANES]
            for first in range(LANES, keys, LANES):
                peak = jnp.maximum(peak, scores[:, :, first : first + LANES])
            peak_ref[span] = peak if step == 0 else jnp.maximum(peak_ref[span], peak)
            return carry

        lax.fori_loop(0, groups, one, 0)

    def take_values(step):
        relay(step, 1).wait_recv()
        block = all_values[pl.ds((z - step) * CORES, CORES)].reshape(keys, value_ref.shape[1])
        for group in range(groups):
            group_values[group, step * keys : (step + 1) * keys, :HEAD_SIZE] = block[
                :, group * HEAD_SIZE : (group + 1) * HEAD_SIZE
            ]

    relay(0, 0).wait_recv()
    score(0)
    for step in range(1, chips):

        @pl.when(z - step >= 0)
        def _():
            for part in (0, 1):
                hop(step - 1, part).wait_recv()
                if step < chips - 1:

                    @pl.when(has_above)
                    def _():
                        hop(step, part).start()

                relay(step, part).start()
            take_values(step - 1)
            relay(step, 0).wait_recv()
            score(step)

        @pl.when(z - step < 0)
        def _():
            @pl.when(z - step == -1)
            def _():
                take_values(step - 1)

            def blank(index, carry):
                score_ref[step, index] = jnp.full((rows, keys), masked_value, jnp.float32)
                return carry

            lax.fori_loop(0, groups * share, blank, 0)

    @pl.when(z == chips - 1)
    def _():
        take_values(chips - 1)

    own = pl.ds(pl.multiple_of(head * own_rows, own_rows), own_rows)
    hidden_rows[...] = hidden_ref[...].T

    def mix(couple, carry):
        group = lax.div(couple * 2, share)
        sinks, tops = [], []
        for member in range(2):
            sinks.append(sink_ref[couple * 2 + member] * log2e)
            peak = jnp.max(peak_ref[couple * 2 + member], axis=-1, keepdims=True)
            tops.append(jnp.maximum(peak, sinks[member]))
        mixed = jnp.zeros((2 * rows, LANES), jnp.float32)
        for step in range(chips):
            weights = jnp.concatenate(
                [
                    jnp.exp2(score_ref[step, couple * 2 + member] - tops[member]).astype(jnp.bfloat16)
                    for member in range(2)
                ],
                axis=0,
            )
            mixed = mixed + jnp.dot(
                weights, group_values[group, step * keys : (step + 1) * keys, :], preferred_element_type=jnp.float32
            )
        both = []
        for member in range(2):
            mine = mixed[member * rows : (member + 1) * rows]
            total = mine[:, HEAD_SIZE : HEAD_SIZE + 1] + jnp.exp2(sinks[member] - tops[member])
            both.append((mine[:, :HEAD_SIZE] / total).astype(jnp.bfloat16))
        span = pl.ds(pl.multiple_of(couple * 2 * HEAD_SIZE, 2 * HEAD_SIZE), 2 * HEAD_SIZE)
        attended_ref[:, span] = jnp.concatenate(both, axis=1)
        return carry

    lax.fori_loop(0, groups * share // 2, mix, 0)

    load.wait()
    spans = column_spans(part_ref.shape[1])
    part_ref[:, spans[-1][0] :] = jnp.zeros((rows, spans[-1][1]), part_ref.dtype)
    sends = {}
    for c, (first, size) in enumerate(spans):
        last = min(first + size, width)
        piece = lax.dot_general(
            attended_ref[...], weight_ref[first:last, :], turned, preferred_element_type=jnp.float32
        )
        part_ref[:, first:last] = piece.astype(jnp.bfloat16)
        for turn, device in enumerate(others):
            target = pl.ds(pl.multiple_of(device["head"] * own_rows, own_rows), own_rows)
            sends[turn, c] = remote(
                part_ref.at[target, pl.ds(first, size)],
                slots.at[turn, :, pl.ds(first, size)],
                head_send.at[turn, c],
                head_recv.at[turn, c],
                device,
            )
            sends[turn, c].start()
    for c, (first, size) in enumerate(spans):
        span = slice(first, min(first + size, width))
        total = hidden_rows[own, span].astype(jnp.float32) + part_ref[own, span].astype(jnp.float32)
        for turn in range(heads - 1):
            sends[turn, c].wait_recv()
            total = total + slots[turn, :, span].astype(jnp.float32)
        out_ref[:, span] = total.astype(jnp.bfloat16)

    for copy in sends.values():
        copy.wait_send()
    for part in (0, 1):
        for step in range(chips):

            @pl.when(z - step >= 0)
            def _():
                relay(step, part).wait_send()
                if step < chips - 1:

                    @pl.when(has_above)
                    def _():
                        hop(step, part).wait_send()


def column_spans(padded):
    wide = 8 * LANES
    return [(first, min(wide, padded - first)) for first in range(0, padded, wide)]


def attend(queries, keys, values, sinks, segments, hidden, w_out):
    chips, heads = lax.axis_size("ctx") // CORES, lax.axis_size("head")
    n_ctx = lax.axis_size("ctx")
    rows = queries.shape[0]
    width = w_out.shape[1]
    padded = -(-width // LANES) * LANES
    groups = keys.shape[1] // HEAD_SIZE
    share = queries.shape[1] // keys.shape[1]
    parts = len(column_spans(padded))
    bf16, f32, dma = jnp.bfloat16, jnp.float32, pltpu.SemaphoreType.DMA
    chip_keys = CORES * rows
    return pl.pallas_call(
        functools.partial(attend_kernel, chips, heads),
        out_shape=jax.ShapeDtypeStruct((rows // heads, width), bf16),
        in_specs=[full_vmem()] * 3
        + [pl.BlockSpec(memory_space=pltpu.SMEM)]
        + [full_vmem()] * 2
        + [pl.BlockSpec(memory_space=pl.ANY)],
        out_specs=full_vmem(),
        scratch_shapes=[
            pltpu.VMEM((n_ctx,) + keys.shape, bf16),
            pltpu.VMEM((n_ctx,) + keys.shape, bf16),
            pltpu.VMEM((groups, share * rows, HEAD_SIZE), bf16),
            pltpu.VMEM((groups, chip_keys, HEAD_SIZE), bf16),
            pltpu.VMEM((groups, chips * chip_keys, LANES), bf16),
            pltpu.VMEM((rows, chip_keys), f32),
            pltpu.VMEM((chips, groups * share, rows, chip_keys), f32),
            pltpu.VMEM((groups * share, rows, LANES), f32),
            pltpu.VMEM(queries.shape, bf16),
            pltpu.VMEM((width, w_out.shape[0]), bf16),
            pltpu.VMEM((rows, width), bf16),
            pltpu.VMEM((rows, padded), bf16),
            pltpu.VMEM((heads - 1, rows // heads, padded), bf16),
            dma((chips, 2)),
            dma((chips, 2)),
            dma((chips, 2)),
            dma((chips, 2)),
            dma((heads - 1, parts)),
            dma((heads - 1, parts)),
            dma(()),
        ],
        compiler_params=pltpu.CompilerParams(
            collective_id=0, has_side_effects=True, vmem_limit_bytes=60 * 1024 * 1024
        ),
        name="attend",
    )(keys, values, queries, sinks, segments.reshape(1, -1), hidden.T, w_out.T)


def layer_kernel(
    chips, heads, experts, tile, columns, residual_ref, gain_ref, router_ref, route_ref, up_hbm, down_hbm,
    out_ref, all_ref, route_rows, lanes_ref, up_ref, down_ref, act_ref, term_ref, got, outgoing, incoming, weight_sem,
    hop_send, hop_recv, copy_send, copy_recv, pair_send, pair_recv, ring_send, ring_recv,
):
    ring = Ring(chips, heads)
    count, half = ring.count, ring.count // 2
    rows, width = out_ref.shape
    start = width % LANES
    chunks = row_chunks(rows)
    parts = range(len(chunks))
    ways = ((0, 1), (1, -1))
    turned = (((1,), (1,)), ((), ()))
    ctx, head = lax.axis_index("ctx"), ring.head

    barrier = pltpu.get_barrier_semaphore()
    peers = [ring.device(1), ring.device(-1), ring.partner]
    for device in peers:
        pl.semaphore_signal(barrier, inc=1, device_id=device, device_id_type=MESH)
    tiles = act_ref.shape[0]

    def load_up(t):
        span = pl.ds(pl.multiple_of(t * tile, 8), tile)
        return [
            pltpu.make_async_copy(up_hbm.at[which, span], up_ref.at[which, span], weight_sem.at[which, t])
            for which in range(2)
        ]

    load_down = pltpu.make_async_copy(down_hbm, down_ref, weight_sem.at[2, 0])
    for t in range(tiles):
        for copy in load_up(t):
            copy.start()
    load_down.start()

    own = pl.ds(pl.multiple_of(head * rows, rows), rows)
    tokens = route_ref.shape[1]
    eye = (
        lax.broadcasted_iota(jnp.int32, (tokens, tokens), 0) == lax.broadcasted_iota(jnp.int32, (tokens, tokens), 1)
    ).astype(jnp.float32)
    route_rows[...] = lax.dot_general(
        eye.astype(jnp.bfloat16),
        route_ref[...].astype(jnp.float32).astype(jnp.bfloat16),
        turned,
        preferred_element_type=jnp.float32,
    )
    lanes_ref[...] = jnp.zeros(lanes_ref.shape, lanes_ref.dtype)
    lanes_ref[start : start + experts, :] = router_ref[...]
    lanes_ref[start + experts : start + 2 * experts, :] = router_ref[...]

    residual = residual_ref[...]
    wide = residual.astype(jnp.float32)
    scale = lax.rsqrt(jnp.mean(wide * wide, axis=-1, keepdims=True) + 1e-05)
    normed = (wide * scale * gain_ref[...][None, :]).astype(jnp.bfloat16)

    logits = lax.dot_general(normed, lanes_ref[...], turned, preferred_element_type=jnp.float32)
    lane = lax.broadcasted_iota(jnp.int32, logits.shape, 1) - start
    first = (lane >= 0) & (lane < experts)
    names = route_rows[own, :]
    present = jnp.zeros(logits.shape, jnp.bool_)
    spot = lane.astype(jnp.float32)
    for k in range(route_ref.shape[0]):
        name = names[:, k : k + 1]
        present = present | (spot == name) | (spot - experts == name)
    top = jnp.max(jnp.where(present, logits, -jnp.inf), axis=-1, keepdims=True)
    powers = jnp.where(present, jnp.exp(jnp.where(present, logits - top, 0.0)), 0.0)
    gates = powers / jnp.sum(jnp.where(first, powers, 0.0), axis=-1, keepdims=True)
    coarse = gates.astype(jnp.bfloat16)
    rest = gates - coarse.astype(jnp.float32)
    tail = jnp.where(first, coarse.astype(jnp.float32), rest)
    mine = ring.block(0, ring.core)
    all_ref[mine, :, width - start :] = tail.astype(jnp.bfloat16)
    all_ref[mine, :, :width] = normed

    def last(index, j):
        return (j == 0) == (index == 0)

    def hop(index, way, step, j):
        view = all_ref.at[ring.block(-way * step, ring.core), chunks[j]]
        return remote(view, view, hop_send.at[index, step, j], hop_recv.at[index, step, j], ring.device(way))

    def relay(slot, offset, j):
        view = all_ref.at[ring.block(offset, ring.core), chunks[j]]
        return remote(view, view, copy_send.at[slot, j], copy_recv.at[slot, j], ring.partner)

    def forward(step, j):
        for index, way in ways:
            if isinstance(step, int) and step == half and not last(index, j):
                continue
            hop(index, way, step - 1, j).wait_recv()
            if last(index, j):
                if not (isinstance(step, int) and step == half):
                    hop(index, way, step, j).start()
            elif not isinstance(step, int):

                @pl.when(step < half - 1)
                def _():
                    hop(index, way, step, j).start()

            elif step < half - 1:
                hop(index, way, step, j).start()
            relay(index * half + step, -way * step, j).start()

    def share(slot, offset):
        return remote(
            term_ref.at[ring.block(offset, 1 - ring.core)], got.at[slot], pair_send.at[slot], pair_recv.at[slot], ring.partner
        )

    def compute(offsets, hooks, fresh=False):
        blocks = [ring.block(offset, core) for offset in offsets for core in range(CORES)]
        used = len(blocks) * rows
        gates = []
        for block in blocks:
            tail = all_ref[block, :, width - start :].astype(jnp.float32)
            lane = lax.broadcasted_iota(jnp.int32, tail.shape, 1) - start
            here = (lane == ctx) | (lane == ctx + experts)
            gates.append(jnp.sum(jnp.where(here, tail, 0.0), axis=1, keepdims=True))
        gate = jnp.concatenate(gates, axis=0)

        def multiply(t, carry):
            if fresh:
                for copy in load_up(t):
                    copy.wait()
            span = pl.ds(pl.multiple_of(t * tile, 8), tile)
            x = jnp.concatenate([all_ref[block, :, :width] for block in blocks], axis=0)
            a = lax.dot_general(x, up_ref[0, span, :], turned, preferred_element_type=jnp.float32)
            b = lax.dot_general(x, up_ref[1, span, :], turned, preferred_element_type=jnp.float32)
            act_ref[t, :used, :] = (a * jax.nn.sigmoid(1.702 * a) * (b + 1.0)).astype(jnp.bfloat16)
            for spot, hook in enumerate(hooks):

                @pl.when(t == min(spot, tiles - 1))
                def _():
                    hook()

            return carry

        lax.fori_loop(0, tiles, multiply, 0)
        if fresh:
            load_down.wait()
        for first in range(0, width, columns):
            span = slice(first, min(first + columns, width))
            piece = 0.0
            for t in range(tiles):
                piece = piece + jnp.dot(
                    act_ref[t, :used, :], down_ref[t * tile : (t + 1) * tile, span], preferred_element_type=jnp.float32
                )
            gated = (piece * gate).astype(jnp.bfloat16)
            for i, block in enumerate(blocks):
                term_ref[block, :, span] = gated[i * rows : (i + 1) * rows]

    pl.semaphore_wait(barrier, len(peers))
    for j in parts:
        for index, way in ways:
            if half > 1 or last(index, j):
                hop(index, way, 0, j).start()
        relay(0, 0, j).start()
    for j in parts:
        relay(0, 0, j).wait_recv()
    compute([0], [], fresh=True)
    share(0, 0).start()
    for j in parts:
        forward(1, j)

    def ready(distance):
        for index, way in ways:
            for j in parts:
                relay(index * half + distance, -way * distance, j).wait_recv()

    def pair_up(distance):
        for index, way in ways:
            share(index * half + distance, -way * distance).start()

    def travel(distance, carry):
        ready(distance)
        compute(
            [-way * distance for index, way in ways], [functools.partial(forward, distance + 1, j) for j in parts]
        )
        pair_up(distance)
        return carry

    lax.fori_loop(1, half - 1, travel, 0)
    ready(half - 1)
    compute([1 - half, half - 1], [functools.partial(forward, half, j) for j in parts])
    pair_up(half - 1)
    arrived = set()

    def slot_of(offset):
        return offset + half if 0 < offset < half else abs(offset)

    def pair(offset, chunk):
        offset = half if offset == -half else offset
        if offset not in arrived:
            share(slot_of(offset), offset).wait_recv()
            arrived.add(offset)
        mine = term_ref[ring.block(offset, ring.core), chunk, :].astype(jnp.float32)
        return mine + got[slot_of(offset), chunk, :].astype(jnp.float32)

    def travelling(index, way, step, j):
        return remote(
            outgoing.at[index, step, chunks[j]],
            incoming.at[index, step, chunks[j]],
            ring_send.at[index, step, j],
            ring_recv.at[index, step, j],
            ring.device(way),
        )

    def ring_step(step, final):
        for j, chunk in enumerate(chunks):
            for index, way in ways:
                if last(index, j) != final:
                    continue
                total = pair(way * (half - step), chunk)
                if step > (0 if final else 1):
                    travelling(index, way, step - 1, j).wait_recv()
                    total = total + incoming[index, step - 1, chunk, :].astype(jnp.float32)
                outgoing[index, step, chunk, :] = total.astype(jnp.bfloat16)
                travelling(index, way, step, j).start()

    ring_step(1, False)
    for j in parts:
        for index, way in ways:
            if last(index, j):
                relay(index * half + half, -way * half, j).wait_recv()
    compute([half], [lambda: None, lambda: None, functools.partial(ring_step, 2, False)])
    share(half, half).start()

    for step in range(half):
        ring_step(step, True)
        if step + 3 < half:
            ring_step(step + 3, False)
    for j, chunk in enumerate(chunks):
        total = pair(0, chunk) + residual_ref[chunk, :].astype(jnp.float32)
        for index, way in ways:
            travelling(index, way, half - 1, j).wait_recv()
            total = total + incoming[index, half - 1, chunk, :].astype(jnp.float32)
        out_ref[chunk, :] = total.astype(jnp.bfloat16)

    for j in parts:
        for index, way in ways:
            for step in range(0 if last(index, j) else 1, half):
                travelling(index, way, step, j).wait_send()
    share(0, 0).wait_send()
    share(half, half).wait_send()
    for j in parts:
        relay(0, 0, j).wait_send()
        for index, way in ways:
            if last(index, j):
                hop(index, way, half - 1, j).wait_send()
                relay(index * half + half, -way * half, j).wait_send()
            hop(index, way, 0, j).wait_send()

    def drain(step, carry):
        for index, way in ways:
            share(index * half + step, -way * step).wait_send()
            for j in parts:
                relay(index * half + step, -way * step, j).wait_send()

                @pl.when(step < half - 1)
                def _():
                    hop(index, way, step, j).wait_send()

        return carry

    lax.fori_loop(1, half, drain, 0)


def norm_and_experts(residual, norm_gain, router, routes, w_gate_up, w_down):
    chips, heads = lax.axis_size("ctx") // CORES, lax.axis_size("head")
    rows, width = residual.shape
    tokens = rows * heads
    experts = router.shape[1]
    hidden_units = w_down.shape[1]
    padded = width - width % LANES + LANES
    half = chips * heads // 2
    blocks = chips * heads * CORES
    parts = len(row_chunks(rows))
    tile = hidden_units // 3 if hidden_units % 48 == 0 else hidden_units
    columns = 8 * LANES
    most = 2 * CORES
    bf16, f32, dma = jnp.bfloat16, jnp.float32, pltpu.SemaphoreType.DMA
    anywhere = pl.BlockSpec(memory_space=pl.ANY)
    return pl.pallas_call(
        functools.partial(layer_kernel, chips, heads, experts, tile, columns),
        out_shape=jax.ShapeDtypeStruct((rows, width), bf16),
        in_specs=[full_vmem()] * 4 + [anywhere] * 2,
        out_specs=full_vmem(),
        scratch_shapes=[
            pltpu.VMEM((blocks, rows, padded), bf16),
            pltpu.VMEM((tokens, routes.shape[1]), f32),
            pltpu.VMEM((LANES, width), bf16),
            pltpu.VMEM((2, hidden_units, width), bf16),
            pltpu.VMEM((hidden_units, width), bf16),
            pltpu.VMEM((hidden_units // tile, most * rows, tile), bf16),
            pltpu.VMEM((blocks, rows, width), bf16),
            pltpu.VMEM((2 * half, rows, width), bf16),
            pltpu.VMEM((2, half, rows, width), bf16),
            pltpu.VMEM((2, half, rows, width), bf16),
            dma((3, hidden_units // tile)),
            dma((2, half, parts)),
            dma((2, half, parts)),
            dma((2 * half + 1, parts)),
            dma((2 * half + 1, parts)),
            dma((2 * half,)),
            dma((2 * half,)),
            dma((2, half, parts)),
            dma((2, half, parts)),
        ],
        compiler_params=pltpu.CompilerParams(
            collective_id=1, has_side_effects=True, vmem_limit_bytes=60 * 1024 * 1024
        ),
        name="norm_and_experts",
    )(
        residual,
        norm_gain,
        router.T,
        routes.T,
        jnp.swapaxes(w_gate_up[0], 1, 2),
        w_down[0],
    )


def body(
    queries,
    keys,
    values,
    sinks,
    segments,
    hidden_in,
    routes,
    w_out,
    norm_gain,
    router,
    w_gate_up,
    w_down,
):
    residual = attend(queries, keys, values, sinks, segments, hidden_in, w_out)
    return norm_and_experts(residual, norm_gain, router, routes, w_gate_up, w_down)


def solution(mesh):
    placed = (
        P(("group", "ctx"), "head"),
        P(("group", "ctx"), "head"),
        P(("group", "ctx"), "head"),
        P("head"),
        P("group"),
        P(("group", "ctx"), None),
        P(("group", "ctx"), None),
        P("head", None),
        P(),
        P(),
        P("ctx", None, None, "head"),
        P("ctx", "head", None),
    )
    return jax.shard_map(
        body,
        mesh=mesh,
        in_specs=placed,
        out_specs=P(("group", "ctx", "head"), None),
        check_vma=False,
    )
```

```python
import functools
import math

import jax
import jax.numpy as jnp
from jax import lax
from jax.experimental import pallas as pl
from jax.experimental.pallas import tpu as pltpu
from jax.sharding import PartitionSpec as P

HEAD_SIZE = 64


masked_value = -1e30


MESH = pl.DeviceIdType.MESH
LANES = 128
CORES = 2


def full_vmem():
    return pl.BlockSpec(memory_space=pltpu.VMEM)


class Ring:
    def __init__(self, chips, heads):
        self.chips, self.heads, self.count = chips, heads, chips * heads
        ctx = lax.axis_index("ctx")
        self.head = lax.axis_index("head")
        self.core = lax.rem(ctx, CORES)
        z = lax.div(ctx, CORES)
        self.place = self.head * chips + z + lax.rem(self.head, 2) * (chips - 1 - 2 * z)
        self.partner = {"ctx": z * CORES + 1 - self.core, "head": self.head}

    def at(self, offset):
        spot = lax.rem(self.place + offset + self.count, self.count)
        head = lax.div(spot, self.chips)
        step = lax.rem(spot, self.chips)
        return head, step + lax.rem(head, 2) * (self.chips - 1 - 2 * step)

    def block(self, offset, core):
        head, z = self.at(offset)
        return (z * CORES + core) * self.heads + head

    def device(self, offset):
        head, z = self.at(offset)
        return {"ctx": z * CORES + self.core, "head": head}


def remote(src, dst, send_sem, recv_sem, device):
    return pltpu.make_async_remote_copy(
        src_ref=src, dst_ref=dst, send_sem=send_sem, recv_sem=recv_sem, device_id=device, device_id_type=MESH
    )


def row_chunks(rows, most):
    count = most if rows % (16 * most) == 0 else 1
    return [pl.ds(first, rows // count) for first in range(0, rows, rows // count)]


def attend_kernel(
    chips, heads, key_ref, value_ref, query_ref, sink_ref, segment_ref, hidden_ref, weight_hbm, out_ref,
    all_keys, all_values, stacked, group_keys, group_values, bias_ref, score_ref, peak_ref, attended_ref, weight_ref,
    hidden_rows, part_ref, slots,
    line_send, line_recv, pair_send, pair_recv, head_send, head_recv, weight_sem,
):
    ctx, head = lax.axis_index("ctx"), lax.axis_index("head")
    z, core = lax.div(ctx, CORES), lax.rem(ctx, CORES)
    rows = query_ref.shape[0]
    groups = key_ref.shape[1] // HEAD_SIZE
    share = query_ref.shape[1] // key_ref.shape[1]
    keys = CORES * rows
    own_rows, width = out_ref.shape
    ins, alls = (key_ref, value_ref), (all_keys, all_values)
    turned = (((1,), (1,)), ((), ()))
    partner = {"ctx": z * CORES + 1 - core}
    above = {"ctx": (z + 1) * CORES + core}
    others = [{"ctx": ctx, "head": lax.rem(head + turn, heads)} for turn in range(1, heads)]
    has_above, has_below = z + 1 < chips, z > 0
    load = pltpu.make_async_copy(weight_hbm, weight_ref, weight_sem)
    load.start()

    barrier = pltpu.get_barrier_semaphore()
    for device in [partner] + others:
        pl.semaphore_signal(barrier, inc=1, device_id=device, device_id_type=MESH)

    @pl.when(has_above)
    def _():
        pl.semaphore_signal(barrier, inc=1, device_id=above, device_id_type=MESH)

    @pl.when(has_below)
    def _():
        pl.semaphore_signal(barrier, inc=1, device_id={"ctx": (z - 1) * CORES + core}, device_id_type=MESH)

    peers = heads + jnp.where(has_above, 1, 0) + jnp.where(has_below, 1, 0)
    pl.semaphore_wait(barrier, peers)

    def hop(step, part):
        block = (z - step) * CORES + core
        source = ins[part] if step == 0 else alls[part].at[block]
        return remote(source, alls[part].at[block], line_send.at[step, part], line_recv.at[step, part], above)

    def relay(step, part):
        block = (z - step) * CORES + core
        source = ins[part] if step == 0 else alls[part].at[block]
        return remote(source, alls[part].at[block], pair_send.at[step, part], pair_recv.at[step, part], partner)

    for part in (0, 1):

        @pl.when(has_above)
        def _():
            hop(0, part).start()

        relay(0, part).start()
    for part in (0, 1):
        alls[part][ctx] = ins[part][...]

    for index in range(groups * share):
        span = slice(index * HEAD_SIZE, (index + 1) * HEAD_SIZE)
        stacked[index // share, index % share * rows : (index % share + 1) * rows, :] = query_ref[:, span]
    lane = lax.broadcasted_iota(jnp.int32, group_values.shape[1:], 1)
    for group in range(groups):
        group_values[group] = (lane == HEAD_SIZE).astype(jnp.float32).astype(jnp.bfloat16)
    here = pl.ds(pl.multiple_of(ctx * rows, rows), rows)
    diagonal = lax.broadcasted_iota(jnp.int32, (rows, rows), 0) == lax.broadcasted_iota(jnp.int32, (rows, rows), 1)
    own_segment = jnp.sum(
        jnp.where(diagonal, segment_ref[:, here].astype(jnp.float32), 0.0), axis=1, keepdims=True
    )
    log2e = math.log2(math.e)
    factor = HEAD_SIZE ** (-0.5) * log2e

    def score(step):
        chip = z - step
        block = all_keys[pl.ds(chip * CORES, CORES)].reshape(keys, key_ref.shape[1])
        for group in range(groups):
            group_keys[group] = block[:, group * HEAD_SIZE : (group + 1) * HEAD_SIZE]
        spot = lax.broadcasted_iota(jnp.int32, (rows, keys), 1) + chip * keys
        place = lax.broadcasted_iota(jnp.int32, (rows, keys), 0) + ctx * rows
        segment = segment_ref[:, pl.ds(pl.multiple_of(chip * keys, keys), keys)].astype(jnp.float32)
        bias_ref[...] = jnp.where((spot <= place) & (segment == own_segment), 0.0, masked_value)

        def one(group, carry):
            scores = lax.dot_general(stacked[group], group_keys[group], turned, preferred_element_type=jnp.float32)
            scores = scores.reshape(share, rows, keys) * factor + bias_ref[...]
            span = pl.ds(group * share, share)
            score_ref[step, span] = scores
            peak = scores[:, :, :LANES]
            for first in range(LANES, keys, LANES):
                peak = jnp.maximum(peak, scores[:, :, first : first + LANES])
            peak_ref[span] = peak if step == 0 else jnp.maximum(peak_ref[span], peak)
            return carry

        lax.fori_loop(0, groups, one, 0)

    def take_values(step):
        relay(step, 1).wait_recv()
        block = all_values[pl.ds((z - step) * CORES, CORES)].reshape(keys, value_ref.shape[1])
        for group in range(groups):
            group_values[group, step * keys : (step + 1) * keys, :HEAD_SIZE] = block[
                :, group * HEAD_SIZE : (group + 1) * HEAD_SIZE
            ]

    relay(0, 0).wait_recv()
    score(0)
    for step in range(1, chips):

        @pl.when(z - step >= 0)
        def _():
            for part in (0, 1):
                hop(step - 1, part).wait_recv()
                if step < chips - 1:

                    @pl.when(has_above)
                    def _():
                        hop(step, part).start()

                relay(step, part).start()
            take_values(step - 1)
            relay(step, 0).wait_recv()
            score(step)

        @pl.when(z - step < 0)
        def _():
            @pl.when(z - step == -1)
            def _():
                take_values(step - 1)

            def blank(index, carry):
                score_ref[step, index] = jnp.full((rows, keys), masked_value, jnp.float32)
                return carry

            lax.fori_loop(0, groups * share, blank, 0)

    @pl.when(z == chips - 1)
    def _():
        take_values(chips - 1)

    own = pl.ds(pl.multiple_of(head * own_rows, own_rows), own_rows)
    hidden_rows[...] = hidden_ref[...].T

    def mix(couple, carry):
        group = lax.div(couple * 2, share)
        sinks, tops = [], []
        for member in range(2):
            sinks.append(sink_ref[couple * 2 + member] * log2e)
            peak = jnp.max(peak_ref[couple * 2 + member], axis=-1, keepdims=True)
            tops.append(jnp.maximum(peak, sinks[member]))
        mixed = jnp.zeros((2 * rows, LANES), jnp.float32)
        for step in range(chips):
            weights = jnp.concatenate(
                [
                    jnp.exp2(score_ref[step, couple * 2 + member] - tops[member]).astype(jnp.bfloat16)
                    for member in range(2)
                ],
                axis=0,
            )
            mixed = mixed + jnp.dot(
                weights, group_values[group, step * keys : (step + 1) * keys, :], preferred_element_type=jnp.float32
            )
        both = []
        for member in range(2):
            mine = mixed[member * rows : (member + 1) * rows]
            total = mine[:, HEAD_SIZE : HEAD_SIZE + 1] + jnp.exp2(sinks[member] - tops[member])
            both.append((mine[:, :HEAD_SIZE] / total).astype(jnp.bfloat16))
        span = pl.ds(pl.multiple_of(couple * 2 * HEAD_SIZE, 2 * HEAD_SIZE), 2 * HEAD_SIZE)
        attended_ref[:, span] = jnp.concatenate(both, axis=1)
        return carry

    lax.fori_loop(0, groups * share // 2, mix, 0, unroll=2)

    load.wait()
    spans = column_spans(part_ref.shape[1])
    part_ref[:, spans[-1][0] :] = jnp.zeros((rows, spans[-1][1]), part_ref.dtype)
    sends = {}
    for c, (first, size) in enumerate(spans):
        last = min(first + size, width)
        piece = lax.dot_general(
            attended_ref[...], weight_ref[first:last, :], turned, preferred_element_type=jnp.float32
        )
        part_ref[:, first:last] = piece.astype(jnp.bfloat16)
        for turn, device in enumerate(others):
            target = pl.ds(pl.multiple_of(device["head"] * own_rows, own_rows), own_rows)
            sends[turn, c] = remote(
                part_ref.at[target, pl.ds(first, size)],
                slots.at[turn, :, pl.ds(first, size)],
                head_send.at[turn, c],
                head_recv.at[turn, c],
                device,
            )
            sends[turn, c].start()
    for c, (first, size) in enumerate(spans):
        span = slice(first, min(first + size, width))
        total = hidden_rows[own, span].astype(jnp.float32) + part_ref[own, span].astype(jnp.float32)
        for turn in range(heads - 1):
            sends[turn, c].wait_recv()
            total = total + slots[turn, :, span].astype(jnp.float32)
        out_ref[:, span] = total.astype(jnp.bfloat16)

    for copy in sends.values():
        copy.wait_send()
    for part in (0, 1):
        for step in range(chips):

            @pl.when(z - step >= 0)
            def _():
                relay(step, part).wait_send()
                if step < chips - 1:

                    @pl.when(has_above)
                    def _():
                        hop(step, part).wait_send()


def column_spans(padded):
    wide = 8 * LANES
    return [(first, min(wide, padded - first)) for first in range(0, padded, wide)]


def attend(queries, keys, values, sinks, segments, hidden, w_out):
    chips, heads = lax.axis_size("ctx") // CORES, lax.axis_size("head")
    n_ctx = lax.axis_size("ctx")
    rows = queries.shape[0]
    width = w_out.shape[1]
    padded = -(-width // LANES) * LANES
    groups = keys.shape[1] // HEAD_SIZE
    share = queries.shape[1] // keys.shape[1]
    parts = len(column_spans(padded))
    bf16, f32, dma = jnp.bfloat16, jnp.float32, pltpu.SemaphoreType.DMA
    chip_keys = CORES * rows
    return pl.pallas_call(
        functools.partial(attend_kernel, chips, heads),
        out_shape=jax.ShapeDtypeStruct((rows // heads, width), bf16),
        in_specs=[full_vmem()] * 3
        + [pl.BlockSpec(memory_space=pltpu.SMEM)]
        + [full_vmem()] * 2
        + [pl.BlockSpec(memory_space=pl.ANY)],
        out_specs=full_vmem(),
        scratch_shapes=[
            pltpu.VMEM((n_ctx,) + keys.shape, bf16),
            pltpu.VMEM((n_ctx,) + keys.shape, bf16),
            pltpu.VMEM((groups, share * rows, HEAD_SIZE), bf16),
            pltpu.VMEM((groups, chip_keys, HEAD_SIZE), bf16),
            pltpu.VMEM((groups, chips * chip_keys, LANES), bf16),
            pltpu.VMEM((rows, chip_keys), f32),
            pltpu.VMEM((chips, groups * share, rows, chip_keys), f32),
            pltpu.VMEM((groups * share, rows, LANES), f32),
            pltpu.VMEM(queries.shape, bf16),
            pltpu.VMEM((width, w_out.shape[0]), bf16),
            pltpu.VMEM((rows, width), bf16),
            pltpu.VMEM((rows, padded), bf16),
            pltpu.VMEM((heads - 1, rows // heads, padded), bf16),
            dma((chips, 2)),
            dma((chips, 2)),
            dma((chips, 2)),
            dma((chips, 2)),
            dma((heads - 1, parts)),
            dma((heads - 1, parts)),
            dma(()),
        ],
        compiler_params=pltpu.CompilerParams(
            collective_id=0, has_side_effects=True, vmem_limit_bytes=60 * 1024 * 1024
        ),
        name="attend",
    )(keys, values, queries, sinks, segments.reshape(1, -1), hidden.T, w_out.T)


def layer_kernel(
    chips, heads, experts, tile, columns, most, residual_ref, gain_ref, router_ref, route_ref, up_hbm, down_hbm,
    out_ref, all_ref, route_rows, lanes_ref, up_ref, down_ref, act_ref, term_ref, got, outgoing, incoming, weight_sem,
    hop_send, hop_recv, copy_send, copy_recv, pair_send, pair_recv, ring_send, ring_recv,
):
    ring = Ring(chips, heads)
    count, half = ring.count, ring.count // 2
    rows, width = out_ref.shape
    start = width % LANES
    chunks, bits = row_chunks(rows, 2), row_chunks(rows, 4)
    parts = range(len(chunks))
    depth = len(bits) // len(chunks)
    order = [part * depth + j for j in range(depth) for part in parts]
    ways = ((0, 1), (1, -1))
    turned = (((1,), (1,)), ((), ()))
    ctx, head = lax.axis_index("ctx"), ring.head

    barrier = pltpu.get_barrier_semaphore()
    peers = [ring.device(1), ring.device(-1), ring.partner]
    for device in peers:
        pl.semaphore_signal(barrier, inc=1, device_id=device, device_id_type=MESH)
    tiles = act_ref.shape[0]

    def load_up(t):
        span = pl.ds(pl.multiple_of(t * tile, 8), tile)
        return [
            pltpu.make_async_copy(up_hbm.at[which, span], up_ref.at[which, span], weight_sem.at[which, t])
            for which in range(2)
        ]

    load_down = pltpu.make_async_copy(down_hbm, down_ref, weight_sem.at[2, 0])
    for t in range(tiles):
        for copy in load_up(t):
            copy.start()
    load_down.start()

    own = pl.ds(pl.multiple_of(head * rows, rows), rows)
    tokens = route_ref.shape[1]
    eye = (
        lax.broadcasted_iota(jnp.int32, (tokens, tokens), 0) == lax.broadcasted_iota(jnp.int32, (tokens, tokens), 1)
    ).astype(jnp.float32)
    route_rows[...] = lax.dot_general(
        eye.astype(jnp.bfloat16),
        route_ref[...].astype(jnp.float32).astype(jnp.bfloat16),
        turned,
        preferred_element_type=jnp.float32,
    )
    lanes_ref[...] = jnp.zeros(lanes_ref.shape, lanes_ref.dtype)
    lanes_ref[start : start + experts, :] = router_ref[...]
    lanes_ref[start + experts : start + 2 * experts, :] = router_ref[...]

    residual = residual_ref[...]
    wide = residual.astype(jnp.float32)
    scale = lax.rsqrt(jnp.mean(wide * wide, axis=-1, keepdims=True) + 1e-05)
    normed = (wide * scale * gain_ref[...][None, :]).astype(jnp.bfloat16)

    logits = lax.dot_general(normed, lanes_ref[...], turned, preferred_element_type=jnp.float32)
    lane = lax.broadcasted_iota(jnp.int32, logits.shape, 1) - start
    first = (lane >= 0) & (lane < experts)
    names = route_rows[own, :]
    present = jnp.zeros(logits.shape, jnp.bool_)
    spot = lane.astype(jnp.float32)
    for k in range(route_ref.shape[0]):
        name = names[:, k : k + 1]
        present = present | (spot == name) | (spot - experts == name)
    top = jnp.max(jnp.where(present, logits, -jnp.inf), axis=-1, keepdims=True)
    powers = jnp.where(present, jnp.exp(jnp.where(present, logits - top, 0.0)), 0.0)
    gates = powers / jnp.sum(jnp.where(first, powers, 0.0), axis=-1, keepdims=True)
    coarse = gates.astype(jnp.bfloat16)
    rest = gates - coarse.astype(jnp.float32)
    tail = jnp.where(first, coarse.astype(jnp.float32), rest)
    mine = ring.block(0, ring.core)
    all_ref[mine, :, width - start :] = tail.astype(jnp.bfloat16)
    all_ref[mine, :, :width] = normed

    def last(index, j):
        return (j == 0) == (index == 0)

    def hop(index, way, step, j):
        view = all_ref.at[ring.block(-way * step, ring.core), chunks[j]]
        return remote(view, view, hop_send.at[index, step, j], hop_recv.at[index, step, j], ring.device(way))

    def relay(slot, offset, j):
        view = all_ref.at[ring.block(offset, ring.core), chunks[j]]
        return remote(view, view, copy_send.at[slot, j], copy_recv.at[slot, j], ring.partner)

    def continues(index, step, j):
        return step < half - 1 or (step == half - 1 and last(index, j))

    def forward(step, j):
        for index, way in ways:
            if continues(index, step - 1, j):
                hop(index, way, step - 1, j).wait_recv()
                if continues(index, step, j):
                    hop(index, way, step, j).start()
                relay(index * half + step, -way * step, j).start()

    def slot_of(offset):
        return offset + half if 0 < offset < half else abs(offset)

    def share(offset):
        slot = slot_of(offset)
        return remote(
            term_ref.at[ring.block(offset, 1 - ring.core)], got.at[slot], pair_send.at[slot], pair_recv.at[slot], ring.partner
        )

    def multiply_blocks(offsets, hooks, fresh):
        blocks = [ring.block(offset, core) for offset in offsets for core in range(CORES)]
        used = len(blocks) * rows
        gates = []
        for block in blocks:
            tail = all_ref[block, :, width - start :].astype(jnp.float32)
            lane = lax.broadcasted_iota(jnp.int32, tail.shape, 1) - start
            here = (lane == ctx) | (lane == ctx + experts)
            gates.append(jnp.sum(jnp.where(here, tail, 0.0), axis=1, keepdims=True))
        gate = jnp.concatenate(gates, axis=0)

        def multiply(t, carry):
            if fresh:
                for copy in load_up(t):
                    copy.wait()
            span = pl.ds(pl.multiple_of(t * tile, 8), tile)
            x = jnp.concatenate([all_ref[block, :, :width] for block in blocks], axis=0)
            a = lax.dot_general(x, up_ref[0, span, :], turned, preferred_element_type=jnp.float32)
            b = lax.dot_general(x, up_ref[1, span, :], turned, preferred_element_type=jnp.float32)
            act_ref[t, :used, :] = (a * jax.nn.sigmoid(1.702 * a) * (b + 1.0)).astype(jnp.bfloat16)
            for spot in range(3):
                if hooks[spot]:

                    @pl.when(t == min(spot, tiles - 1))
                    def _():
                        for hook in hooks[spot]:
                            hook()

            return carry

        lax.fori_loop(0, tiles, multiply, 0)
        if fresh:
            load_down.wait()
        for first in range(0, width, columns):
            span = slice(first, min(first + columns, width))
            piece = 0.0
            for t in range(tiles):
                piece = piece + jnp.dot(
                    act_ref[t, :used, :], down_ref[t * tile : (t + 1) * tile, span], preferred_element_type=jnp.float32
                )
            gated = (piece * gate).astype(jnp.bfloat16)
            for i, block in enumerate(blocks):
                term_ref[block, :, span] = gated[i * rows : (i + 1) * rows]
            if first == columns:
                for hook in hooks[3]:
                    hook()

    def experts_on(offsets, hooks=((), (), (), ()), fresh=False):
        for offset in offsets:
            for index, way in ways:
                for j in parts:
                    distance = abs(offset)
                    if offset == 0:
                        if index == 0:
                            relay(0, 0, j).wait_recv()
                    elif continues(index, distance - 1, j) and (distance == half or offset == -way * distance):
                        relay(index * half + distance, -way * distance, j).wait_recv()
        for first in range(0, len(offsets), most):
            multiply_blocks(offsets[first : first + most], hooks, fresh)
            hooks, fresh = ((), (), (), ()), False
        for offset in offsets:
            share(offset).start()

    arrived = set()

    def pair(offset, bit):
        offset = half if offset == -half else offset
        if offset not in arrived:
            share(offset).wait_recv()
            arrived.add(offset)
        mine = term_ref[ring.block(offset, ring.core), bits[bit], :].astype(jnp.float32)
        return mine + got[slot_of(offset), bits[bit], :].astype(jnp.float32)

    def travelling(index, way, step, bit):
        return remote(
            outgoing.at[index, step, bits[bit]],
            incoming.at[index, step, bits[bit]],
            ring_send.at[index, step, bit],
            ring_recv.at[index, step, bit],
            ring.device(way),
        )

    def ring_step(final, step, bit):
        for index, way in ways:
            if last(index, bit // depth) == final:
                total = pair(way * (half - step), bit)
                if step > (0 if final else 1):
                    travelling(index, way, step - 1, bit).wait_recv()
                    total = total + incoming[index, step - 1, bits[bit], :].astype(jnp.float32)
                outgoing[index, step, bits[bit], :] = total.astype(jnp.bfloat16)
                travelling(index, way, step, bit).start()

    def finish(bit):
        total = pair(0, bit) + residual_ref[bits[bit], :].astype(jnp.float32)
        for index, way in ways:
            travelling(index, way, half - 1, bit).wait_recv()
            total = total + incoming[index, half - 1, bits[bit], :].astype(jnp.float32)
        out_ref[bits[bit], :] = total.astype(jnp.bfloat16)

    def gather(step, j):
        return functools.partial(forward, step, j)

    def short(step, bit):
        return functools.partial(ring_step, False, step, bit)

    pl.semaphore_wait(barrier, len(peers))
    for j in parts:
        for index, way in ways:
            if continues(index, 0, j):
                hop(index, way, 0, j).start()
        relay(0, 0, j).start()
    if depth == 2 and half == 4:
        experts_on([0], ((), (), [gather(1, 0)], ()), fresh=True)
        forward(1, 1)
        experts_on([1, -1], ((), [gather(2, 0)], (), ()))
        forward(2, 1)
        experts_on([2, -2], ((), [gather(3, 0)], (), [gather(3, 1)]))
        experts_on([3, -3], ((), [gather(4, 0), gather(4, 1)], (), ()))
        for bit in order:
            ring_step(False, 1, bit)
        experts_on([4], ((), (), [short(2, 0), short(2, 2)], [short(2, 1), short(2, 3)]))
        for bit in order:
            ring_step(True, 0, bit)
        for bit in order:
            ring_step(False, 3, bit)
        for step in (1, 2, 3):
            for bit in order:
                ring_step(True, step, bit)
    else:
        for step in range(1, half + 1):
            for j in parts:
                forward(step, j)
        offsets = [0]
        for distance in range(1, half):
            offsets += [distance, -distance]
        experts_on(offsets + [half], fresh=True)
        for step in range(half):
            for bit in order:
                ring_step(True, step, bit)
                if step > 0:
                    ring_step(False, step, bit)
    for bit in order:
        finish(bit)

    for offset in range(1 - half, half + 1):
        share(offset).wait_send()
    for j in parts:
        relay(0, 0, j).wait_send()
    for index, way in ways:
        for step in range(half):
            for j in parts:
                if continues(index, step, j):
                    hop(index, way, step, j).wait_send()
                    relay(index * half + step + 1, -way * (step + 1), j).wait_send()
            for bit in order:
                if step > 0 or last(index, bit // depth):
                    travelling(index, way, step, bit).wait_send()


def norm_and_experts(residual, norm_gain, router, routes, w_gate_up, w_down):
    chips, heads = lax.axis_size("ctx") // CORES, lax.axis_size("head")
    rows, width = residual.shape
    tokens = rows * heads
    experts = router.shape[1]
    hidden_units = w_down.shape[1]
    padded = width - width % LANES + LANES
    half = chips * heads // 2
    blocks = chips * heads * CORES
    parts, bits = len(row_chunks(rows, 2)), len(row_chunks(rows, 4))
    tile = hidden_units // 3 if hidden_units % 48 == 0 else hidden_units
    columns = 8 * LANES
    most = 2
    bf16, f32, dma = jnp.bfloat16, jnp.float32, pltpu.SemaphoreType.DMA
    anywhere = pl.BlockSpec(memory_space=pl.ANY)
    return pl.pallas_call(
        functools.partial(layer_kernel, chips, heads, experts, tile, columns, most),
        out_shape=jax.ShapeDtypeStruct((rows, width), bf16),
        in_specs=[full_vmem()] * 4 + [anywhere] * 2,
        out_specs=full_vmem(),
        scratch_shapes=[
            pltpu.VMEM((blocks, rows, padded), bf16),
            pltpu.VMEM((tokens, routes.shape[1]), f32),
            pltpu.VMEM((LANES, width), bf16),
            pltpu.VMEM((2, hidden_units, width), bf16),
            pltpu.VMEM((hidden_units, width), bf16),
            pltpu.VMEM((hidden_units // tile, most * CORES * rows, tile), bf16),
            pltpu.VMEM((blocks, rows, width), bf16),
            pltpu.VMEM((2 * half, rows, width), bf16),
            pltpu.VMEM((2, half, rows, width), bf16),
            pltpu.VMEM((2, half, rows, width), bf16),
            dma((3, hidden_units // tile)),
            dma((2, half, parts)),
            dma((2, half, parts)),
            dma((2 * half + 1, parts)),
            dma((2 * half + 1, parts)),
            dma((2 * half,)),
            dma((2 * half,)),
            dma((2, half, bits)),
            dma((2, half, bits)),
        ],
        compiler_params=pltpu.CompilerParams(
            collective_id=1, has_side_effects=True, vmem_limit_bytes=60 * 1024 * 1024
        ),
        name="norm_and_experts",
    )(
        residual,
        norm_gain,
        router.T,
        routes.T,
        jnp.swapaxes(w_gate_up[0], 1, 2),
        w_down[0],
    )


def body(
    queries,
    keys,
    values,
    sinks,
    segments,
    hidden_in,
    routes,
    w_out,
    norm_gain,
    router,
    w_gate_up,
    w_down,
):
    residual = attend(queries, keys, values, sinks, segments, hidden_in, w_out)
    return norm_and_experts(residual, norm_gain, router, routes, w_gate_up, w_down)


def solution(mesh):
    placed = (
        P(("group", "ctx"), "head"),
        P(("group", "ctx"), "head"),
        P(("group", "ctx"), "head"),
        P("head"),
        P("group"),
        P(("group", "ctx"), None),
        P(("group", "ctx"), None),
        P("head", None),
        P(),
        P(),
        P("ctx", None, None, "head"),
        P("ctx", "head", None),
    )
    return jax.shard_map(
        body,
        mesh=mesh,
        in_specs=placed,
        out_specs=P(("group", "ctx", "head"), None),
        check_vma=False,
    )
```

```python
import functools
import math

import jax
import jax.numpy as jnp
from jax import lax
from jax.experimental import pallas as pl
from jax.experimental.pallas import tpu as pltpu
from jax.sharding import PartitionSpec as P

HEAD_SIZE = 64


masked_value = -1e30


MESH = pl.DeviceIdType.MESH
LANES = 128
CORES = 2


def full_vmem():
    return pl.BlockSpec(memory_space=pltpu.VMEM)


class Ring:
    def __init__(self, chips, heads):
        self.chips, self.heads, self.count = chips, heads, chips * heads
        ctx = lax.axis_index("ctx")
        self.head = lax.axis_index("head")
        self.core = lax.rem(ctx, CORES)
        z = lax.div(ctx, CORES)
        self.place = self.head * chips + z + lax.rem(self.head, 2) * (chips - 1 - 2 * z)
        self.partner = {"ctx": z * CORES + 1 - self.core, "head": self.head}

    def at(self, offset):
        spot = lax.rem(self.place + offset + self.count, self.count)
        head = lax.div(spot, self.chips)
        step = lax.rem(spot, self.chips)
        return head, step + lax.rem(head, 2) * (self.chips - 1 - 2 * step)

    def block(self, offset, core):
        head, z = self.at(offset)
        return (z * CORES + core) * self.heads + head

    def device(self, offset):
        head, z = self.at(offset)
        return {"ctx": z * CORES + self.core, "head": head}


def remote(src, dst, send_sem, recv_sem, device):
    return pltpu.make_async_remote_copy(
        src_ref=src, dst_ref=dst, send_sem=send_sem, recv_sem=recv_sem, device_id=device, device_id_type=MESH
    )


def row_chunks(rows, most):
    count = most if rows % (16 * most) == 0 else 1
    return [pl.ds(first, rows // count) for first in range(0, rows, rows // count)]


def attend_kernel(
    chips, heads, key_ref, value_ref, query_ref, sink_ref, segment_ref, hidden_ref, weight_hbm, out_ref,
    all_keys, all_values, stacked, group_keys, group_values, bias_ref, score_ref, peak_ref, attended_ref, weight_ref,
    hidden_rows, part_ref, slots,
    line_send, line_recv, pair_send, pair_recv, head_send, head_recv, weight_sem,
):
    ctx, head = lax.axis_index("ctx"), lax.axis_index("head")
    z, core = lax.div(ctx, CORES), lax.rem(ctx, CORES)
    rows = query_ref.shape[0]
    groups = key_ref.shape[1] // HEAD_SIZE
    share = query_ref.shape[1] // key_ref.shape[1]
    keys = CORES * rows
    own_rows, width = out_ref.shape
    ins, alls = (key_ref, value_ref), (all_keys, all_values)
    turned = (((1,), (1,)), ((), ()))
    partner = {"ctx": z * CORES + 1 - core}
    above = {"ctx": (z + 1) * CORES + core}
    others = [{"ctx": ctx, "head": lax.rem(head + turn, heads)} for turn in range(1, heads)]
    has_above, has_below = z + 1 < chips, z > 0
    load = pltpu.make_async_copy(weight_hbm, weight_ref, weight_sem)
    load.start()

    barrier = pltpu.get_barrier_semaphore()
    for device in [partner] + others:
        pl.semaphore_signal(barrier, inc=1, device_id=device, device_id_type=MESH)

    @pl.when(has_above)
    def _():
        pl.semaphore_signal(barrier, inc=1, device_id=above, device_id_type=MESH)

    @pl.when(has_below)
    def _():
        pl.semaphore_signal(barrier, inc=1, device_id={"ctx": (z - 1) * CORES + core}, device_id_type=MESH)

    peers = heads + jnp.where(has_above, 1, 0) + jnp.where(has_below, 1, 0)
    pl.semaphore_wait(barrier, peers)

    def hop(step, part):
        block = (z - step) * CORES + core
        source = ins[part] if step == 0 else alls[part].at[block]
        return remote(source, alls[part].at[block], line_send.at[step, part], line_recv.at[step, part], above)

    def relay(step, part):
        block = (z - step) * CORES + core
        source = ins[part] if step == 0 else alls[part].at[block]
        return remote(source, alls[part].at[block], pair_send.at[step, part], pair_recv.at[step, part], partner)

    for part in (0, 1):

        @pl.when(has_above)
        def _():
            hop(0, part).start()

        relay(0, part).start()
    for part in (0, 1):
        alls[part][ctx] = ins[part][...]

    for index in range(groups * share):
        span = slice(index * HEAD_SIZE, (index + 1) * HEAD_SIZE)
        stacked[index // share, index % share * rows : (index % share + 1) * rows, :] = query_ref[:, span]
    lane = lax.broadcasted_iota(jnp.int32, group_values.shape[1:], 1)
    for group in range(groups):
        group_values[group] = (lane == HEAD_SIZE).astype(jnp.float32).astype(jnp.bfloat16)
    here = pl.ds(pl.multiple_of(ctx * rows, rows), rows)
    diagonal = lax.broadcasted_iota(jnp.int32, (rows, rows), 0) == lax.broadcasted_iota(jnp.int32, (rows, rows), 1)
    own_segment = jnp.sum(
        jnp.where(diagonal, segment_ref[:, here].astype(jnp.float32), 0.0), axis=1, keepdims=True
    )
    log2e = math.log2(math.e)
    factor = HEAD_SIZE ** (-0.5) * log2e

    def score(step):
        chip = z - step
        block = all_keys[pl.ds(chip * CORES, CORES)].reshape(keys, key_ref.shape[1])
        for group in range(groups):
            group_keys[group] = block[:, group * HEAD_SIZE : (group + 1) * HEAD_SIZE]
        spot = lax.broadcasted_iota(jnp.int32, (rows, keys), 1) + chip * keys
        place = lax.broadcasted_iota(jnp.int32, (rows, keys), 0) + ctx * rows
        segment = segment_ref[:, pl.ds(pl.multiple_of(chip * keys, keys), keys)].astype(jnp.float32)
        bias_ref[...] = jnp.where((spot <= place) & (segment == own_segment), 0.0, masked_value)

        def one(group, carry):
            scores = lax.dot_general(stacked[group], group_keys[group], turned, preferred_element_type=jnp.float32)
            scores = scores.reshape(share, rows, keys) * factor + bias_ref[...]
            span = pl.ds(group * share, share)
            score_ref[step, span] = scores
            peak = scores[:, :, :LANES]
            for first in range(LANES, keys, LANES):
                peak = jnp.maximum(peak, scores[:, :, first : first + LANES])
            peak_ref[span] = peak if step == 0 else jnp.maximum(peak_ref[span], peak)
            return carry

        lax.fori_loop(0, groups, one, 0, unroll=2)

    def take_values(step):
        relay(step, 1).wait_recv()
        block = all_values[pl.ds((z - step) * CORES, CORES)].reshape(keys, value_ref.shape[1])
        for group in range(groups):
            group_values[group, step * keys : (step + 1) * keys, :HEAD_SIZE] = block[
                :, group * HEAD_SIZE : (group + 1) * HEAD_SIZE
            ]

    hidden_rows[...] = hidden_ref[...].T
    relay(0, 0).wait_recv()
    score(0)
    for step in range(1, chips):

        @pl.when(z - step >= 0)
        def _():
            for part in (0, 1):
                hop(step - 1, part).wait_recv()
                if step < chips - 1:

                    @pl.when(has_above)
                    def _():
                        hop(step, part).start()

                relay(step, part).start()
            take_values(step - 1)
            relay(step, 0).wait_recv()
            score(step)

        @pl.when(z - step < 0)
        def _():
            @pl.when(z - step == -1)
            def _():
                take_values(step - 1)

            def blank(index, carry):
                score_ref[step, index] = jnp.full((rows, keys), masked_value, jnp.float32)
                return carry

            lax.fori_loop(0, groups * share, blank, 0)

    @pl.when(z == chips - 1)
    def _():
        take_values(chips - 1)

    own = pl.ds(pl.multiple_of(head * own_rows, own_rows), own_rows)

    def mix(couple, carry):
        group = lax.div(couple * 2, share)
        sinks, tops = [], []
        for member in range(2):
            sinks.append(sink_ref[couple * 2 + member] * log2e)
            peak = jnp.max(peak_ref[couple * 2 + member], axis=-1, keepdims=True)
            tops.append(jnp.maximum(peak, sinks[member]))
        mixed = jnp.zeros((2 * rows, LANES), jnp.float32)
        for step in range(chips):
            weights = jnp.concatenate(
                [
                    jnp.exp2(score_ref[step, couple * 2 + member] - tops[member]).astype(jnp.bfloat16)
                    for member in range(2)
                ],
                axis=0,
            )
            mixed = mixed + jnp.dot(
                weights, group_values[group, step * keys : (step + 1) * keys, :], preferred_element_type=jnp.float32
            )
        both = []
        for member in range(2):
            mine = mixed[member * rows : (member + 1) * rows]
            total = mine[:, HEAD_SIZE : HEAD_SIZE + 1] + jnp.exp2(sinks[member] - tops[member])
            both.append((mine[:, :HEAD_SIZE] / total).astype(jnp.bfloat16))
        span = pl.ds(pl.multiple_of(couple * 2 * HEAD_SIZE, 2 * HEAD_SIZE), 2 * HEAD_SIZE)
        attended_ref[:, span] = jnp.concatenate(both, axis=1)
        return carry

    lax.fori_loop(0, groups * share // 2, mix, 0, unroll=4)

    load.wait()
    spans = column_spans(part_ref.shape[1])
    part_ref[:, spans[-1][0] :] = jnp.zeros((rows, spans[-1][1]), part_ref.dtype)
    sends = {}
    for c, (first, size) in enumerate(spans):
        last = min(first + size, width)
        piece = lax.dot_general(
            attended_ref[...], weight_ref[first:last, :], turned, preferred_element_type=jnp.float32
        )
        part_ref[:, first:last] = piece.astype(jnp.bfloat16)
        for turn, device in enumerate(others):
            target = pl.ds(pl.multiple_of(device["head"] * own_rows, own_rows), own_rows)
            sends[turn, c] = remote(
                part_ref.at[target, pl.ds(first, size)],
                slots.at[turn, :, pl.ds(first, size)],
                head_send.at[turn, c],
                head_recv.at[turn, c],
                device,
            )
            sends[turn, c].start()
    for c, (first, size) in enumerate(spans):
        span = slice(first, min(first + size, width))
        total = hidden_rows[own, span].astype(jnp.float32) + part_ref[own, span].astype(jnp.float32)
        for turn in range(heads - 1):
            sends[turn, c].wait_recv()
            total = total + slots[turn, :, span].astype(jnp.float32)
        out_ref[:, span] = total.astype(jnp.bfloat16)

    for copy in sends.values():
        copy.wait_send()
    for part in (0, 1):
        for step in range(chips):

            @pl.when(z - step >= 0)
            def _():
                relay(step, part).wait_send()
                if step < chips - 1:

                    @pl.when(has_above)
                    def _():
                        hop(step, part).wait_send()


def column_spans(padded):
    wide = 4 * LANES
    return [(first, min(wide, padded - first)) for first in range(0, padded, wide)]


def attend(queries, keys, values, sinks, segments, hidden, w_out):
    chips, heads = lax.axis_size("ctx") // CORES, lax.axis_size("head")
    n_ctx = lax.axis_size("ctx")
    rows = queries.shape[0]
    width = w_out.shape[1]
    padded = -(-width // LANES) * LANES
    groups = keys.shape[1] // HEAD_SIZE
    share = queries.shape[1] // keys.shape[1]
    parts = len(column_spans(padded))
    bf16, f32, dma = jnp.bfloat16, jnp.float32, pltpu.SemaphoreType.DMA
    chip_keys = CORES * rows
    return pl.pallas_call(
        functools.partial(attend_kernel, chips, heads),
        out_shape=jax.ShapeDtypeStruct((rows // heads, width), bf16),
        in_specs=[full_vmem()] * 3
        + [pl.BlockSpec(memory_space=pltpu.SMEM)]
        + [full_vmem()] * 2
        + [pl.BlockSpec(memory_space=pl.ANY)],
        out_specs=full_vmem(),
        scratch_shapes=[
            pltpu.VMEM((n_ctx,) + keys.shape, bf16),
            pltpu.VMEM((n_ctx,) + keys.shape, bf16),
            pltpu.VMEM((groups, share * rows, HEAD_SIZE), bf16),
            pltpu.VMEM((groups, chip_keys, HEAD_SIZE), bf16),
            pltpu.VMEM((groups, chips * chip_keys, LANES), bf16),
            pltpu.VMEM((rows, chip_keys), f32),
            pltpu.VMEM((chips, groups * share, rows, chip_keys), f32),
            pltpu.VMEM((groups * share, rows, LANES), f32),
            pltpu.VMEM(queries.shape, bf16),
            pltpu.VMEM((width, w_out.shape[0]), bf16),
            pltpu.VMEM((rows, width), bf16),
            pltpu.VMEM((rows, padded), bf16),
            pltpu.VMEM((heads - 1, rows // heads, padded), bf16),
            dma((chips, 2)),
            dma((chips, 2)),
            dma((chips, 2)),
            dma((chips, 2)),
            dma((heads - 1, parts)),
            dma((heads - 1, parts)),
            dma(()),
        ],
        compiler_params=pltpu.CompilerParams(
            collective_id=0, has_side_effects=True, vmem_limit_bytes=60 * 1024 * 1024
        ),
        name="attend",
    )(keys, values, queries, sinks, segments.reshape(1, -1), hidden.T, w_out.T)


def layer_kernel(
    chips, heads, experts, tile, columns, most, residual_ref, gain_ref, router_ref, route_ref, up_hbm, down_hbm,
    out_ref, all_ref, route_rows, lanes_ref, up_ref, down_ref, act_ref, term_ref, got, outgoing, incoming, weight_sem,
    hop_send, hop_recv, copy_send, copy_recv, pair_send, pair_recv, ring_send, ring_recv,
):
    ring = Ring(chips, heads)
    count, half = ring.count, ring.count // 2
    rows, width = out_ref.shape
    start = width % LANES
    chunks, bits = row_chunks(rows, 2), row_chunks(rows, 4)
    parts = range(len(chunks))
    depth = len(bits) // len(chunks)
    order = [part * depth + j for j in range(depth) for part in parts]
    ways = ((0, 1), (1, -1))
    turned = (((1,), (1,)), ((), ()))
    ctx, head = lax.axis_index("ctx"), ring.head

    barrier = pltpu.get_barrier_semaphore()
    peers = [ring.device(1), ring.device(-1), ring.partner]
    for device in peers:
        pl.semaphore_signal(barrier, inc=1, device_id=device, device_id_type=MESH)
    tiles = act_ref.shape[0]

    def load_up(t):
        span = pl.ds(pl.multiple_of(t * tile, 8), tile)
        return [
            pltpu.make_async_copy(up_hbm.at[which, span], up_ref.at[which, span], weight_sem.at[which, t])
            for which in range(2)
        ]

    load_down = pltpu.make_async_copy(down_hbm, down_ref, weight_sem.at[2, 0])
    for t in range(tiles):
        for copy in load_up(t):
            copy.start()
    load_down.start()

    own = pl.ds(pl.multiple_of(head * rows, rows), rows)
    tokens = route_ref.shape[1]
    eye = (
        lax.broadcasted_iota(jnp.int32, (tokens, tokens), 0) == lax.broadcasted_iota(jnp.int32, (tokens, tokens), 1)
    ).astype(jnp.float32)
    route_rows[...] = lax.dot_general(
        eye.astype(jnp.bfloat16),
        route_ref[...].astype(jnp.float32).astype(jnp.bfloat16),
        turned,
        preferred_element_type=jnp.float32,
    )
    lanes_ref[...] = jnp.zeros(lanes_ref.shape, lanes_ref.dtype)
    lanes_ref[start : start + experts, :] = router_ref[...]
    lanes_ref[start + experts : start + 2 * experts, :] = router_ref[...]

    residual = residual_ref[...]
    wide = residual.astype(jnp.float32)
    scale = lax.rsqrt(jnp.mean(wide * wide, axis=-1, keepdims=True) + 1e-05)
    normed = (wide * scale * gain_ref[...][None, :]).astype(jnp.bfloat16)

    logits = lax.dot_general(normed, lanes_ref[...], turned, preferred_element_type=jnp.float32)
    lane = lax.broadcasted_iota(jnp.int32, logits.shape, 1) - start
    first = (lane >= 0) & (lane < experts)
    names = route_rows[own, :]
    present = jnp.zeros(logits.shape, jnp.bool_)
    spot = lane.astype(jnp.float32)
    for k in range(route_ref.shape[0]):
        name = names[:, k : k + 1]
        present = present | (spot == name) | (spot - experts == name)
    top = jnp.max(jnp.where(present, logits, -jnp.inf), axis=-1, keepdims=True)
    powers = jnp.where(present, jnp.exp(jnp.where(present, logits - top, 0.0)), 0.0)
    gates = powers / jnp.sum(jnp.where(first, powers, 0.0), axis=-1, keepdims=True)
    coarse = gates.astype(jnp.bfloat16)
    rest = gates - coarse.astype(jnp.float32)
    tail = jnp.where(first, coarse.astype(jnp.float32), rest)
    mine = ring.block(0, ring.core)
    all_ref[mine, :, width - start :] = tail.astype(jnp.bfloat16)
    all_ref[mine, :, :width] = normed

    def last(index, j):
        return (j == 0) == (index == 0)

    def hop(index, way, step, j):
        view = all_ref.at[ring.block(-way * step, ring.core), chunks[j]]
        return remote(view, view, hop_send.at[index, step, j], hop_recv.at[index, step, j], ring.device(way))

    def relay(slot, offset, j):
        view = all_ref.at[ring.block(offset, ring.core), chunks[j]]
        return remote(view, view, copy_send.at[slot, j], copy_recv.at[slot, j], ring.partner)

    def continues(index, step, j):
        return step < half - 1 or (step == half - 1 and last(index, j))

    def forward(step, j):
        for index, way in ways:
            if continues(index, step - 1, j):
                hop(index, way, step - 1, j).wait_recv()
                if continues(index, step, j):
                    hop(index, way, step, j).start()
                relay(index * half + step, -way * step, j).start()

    def slot_of(offset):
        return offset + half if 0 < offset < half else abs(offset)

    def share(offset):
        slot = slot_of(offset)
        return remote(
            term_ref.at[ring.block(offset, 1 - ring.core)], got.at[slot], pair_send.at[slot], pair_recv.at[slot], ring.partner
        )

    def multiply_blocks(offsets, hooks, fresh):
        blocks = [ring.block(offset, core) for offset in offsets for core in range(CORES)]
        used = len(blocks) * rows
        gates = []
        for block in blocks:
            tail = all_ref[block, :, width - start :].astype(jnp.float32)
            lane = lax.broadcasted_iota(jnp.int32, tail.shape, 1) - start
            here = (lane == ctx) | (lane == ctx + experts)
            gates.append(jnp.sum(jnp.where(here, tail, 0.0), axis=1, keepdims=True))
        gate = jnp.concatenate(gates, axis=0)

        def multiply(t, carry):
            if fresh:
                for copy in load_up(t):
                    copy.wait()
            span = pl.ds(pl.multiple_of(t * tile, 8), tile)
            x = jnp.concatenate([all_ref[block, :, :width] for block in blocks], axis=0)
            a = lax.dot_general(x, up_ref[0, span, :], turned, preferred_element_type=jnp.float32)
            b = lax.dot_general(x, up_ref[1, span, :], turned, preferred_element_type=jnp.float32)
            act_ref[t, :used, :] = (a * jax.nn.sigmoid(1.702 * a) * (b + 1.0)).astype(jnp.bfloat16)
            for spot in range(3):
                if hooks[spot]:

                    @pl.when(t == min(spot, tiles - 1))
                    def _():
                        for hook in hooks[spot]:
                            hook()

            return carry

        lax.fori_loop(0, tiles, multiply, 0)
        if fresh:
            load_down.wait()
        for first in range(0, width, columns):
            span = slice(first, min(first + columns, width))
            piece = 0.0
            for t in range(tiles):
                piece = piece + jnp.dot(
                    act_ref[t, :used, :], down_ref[t * tile : (t + 1) * tile, span], preferred_element_type=jnp.float32
                )
            gated = (piece * gate).astype(jnp.bfloat16)
            for i, block in enumerate(blocks):
                term_ref[block, :, span] = gated[i * rows : (i + 1) * rows]
            if first == columns:
                for hook in hooks[3]:
                    hook()

    def experts_on(offsets, hooks=((), (), (), ()), fresh=False):
        for offset in offsets:
            for index, way in ways:
                for j in parts:
                    distance = abs(offset)
                    if offset == 0:
                        if index == 0:
                            relay(0, 0, j).wait_recv()
                    elif continues(index, distance - 1, j) and (distance == half or offset == -way * distance):
                        relay(index * half + distance, -way * distance, j).wait_recv()
        for first in range(0, len(offsets), most):
            multiply_blocks(offsets[first : first + most], hooks, fresh)
            hooks, fresh = ((), (), (), ()), False
        for offset in offsets:
            share(offset).start()

    arrived = set()

    def pair(offset, bit):
        offset = half if offset == -half else offset
        if offset not in arrived:
            share(offset).wait_recv()
            arrived.add(offset)
        mine = term_ref[ring.block(offset, ring.core), bits[bit], :].astype(jnp.float32)
        return mine + got[slot_of(offset), bits[bit], :].astype(jnp.float32)

    def travelling(index, way, step, bit):
        return remote(
            outgoing.at[index, step, bits[bit]],
            incoming.at[index, step, bits[bit]],
            ring_send.at[index, step, bit],
            ring_recv.at[index, step, bit],
            ring.device(way),
        )

    def ring_step(final, step, bit):
        for index, way in ways:
            if last(index, bit // depth) == final:
                total = pair(way * (half - step), bit)
                if step > (0 if final else 1):
                    travelling(index, way, step - 1, bit).wait_recv()
                    total = total + incoming[index, step - 1, bits[bit], :].astype(jnp.float32)
                outgoing[index, step, bits[bit], :] = total.astype(jnp.bfloat16)
                travelling(index, way, step, bit).start()

    def finish(bit):
        total = pair(0, bit) + residual_ref[bits[bit], :].astype(jnp.float32)
        for index, way in ways:
            travelling(index, way, half - 1, bit).wait_recv()
            total = total + incoming[index, half - 1, bits[bit], :].astype(jnp.float32)
        out_ref[bits[bit], :] = total.astype(jnp.bfloat16)

    def gather(step, j):
        return functools.partial(forward, step, j)

    def short(step, bit):
        return functools.partial(ring_step, False, step, bit)

    pl.semaphore_wait(barrier, len(peers))
    for j in parts:
        for index, way in ways:
            if continues(index, 0, j):
                hop(index, way, 0, j).start()
        relay(0, 0, j).start()
    if depth == 2 and half == 4:
        experts_on([0], ((), (), [gather(1, 0)], ()), fresh=True)
        forward(1, 1)
        experts_on([1, -1], ((), [gather(2, 0)], (), [gather(2, 1)]))
        experts_on([2, -2], ((), [gather(3, 0)], (), [gather(3, 1)]))
        experts_on([3, -3], ((), [gather(4, 0), gather(4, 1)], (), ()))
        for bit in order:
            ring_step(False, 1, bit)
        experts_on([4], ((), (), [short(2, 0), short(2, 2)], [short(2, 1), short(2, 3)]))
        for bit in order:
            ring_step(True, 0, bit)
        for bit in order:
            ring_step(False, 3, bit)
        for step in (1, 2, 3):
            for bit in order:
                ring_step(True, step, bit)
    else:
        for step in range(1, half + 1):
            for j in parts:
                forward(step, j)
        offsets = [0]
        for distance in range(1, half):
            offsets += [distance, -distance]
        experts_on(offsets + [half], fresh=True)
        for step in range(half):
            for bit in order:
                ring_step(True, step, bit)
                if step > 0:
                    ring_step(False, step, bit)
    for bit in order:
        finish(bit)

    for offset in range(1 - half, half + 1):
        share(offset).wait_send()
    for j in parts:
        relay(0, 0, j).wait_send()
    for index, way in ways:
        for step in range(half):
            for j in parts:
                if continues(index, step, j):
                    hop(index, way, step, j).wait_send()
                    relay(index * half + step + 1, -way * (step + 1), j).wait_send()
            for bit in order:
                if step > 0 or last(index, bit // depth):
                    travelling(index, way, step, bit).wait_send()


def norm_and_experts(residual, norm_gain, router, routes, w_gate_up, w_down):
    chips, heads = lax.axis_size("ctx") // CORES, lax.axis_size("head")
    rows, width = residual.shape
    tokens = rows * heads
    experts = router.shape[1]
    hidden_units = w_down.shape[1]
    padded = width - width % LANES + LANES
    half = chips * heads // 2
    blocks = chips * heads * CORES
    parts, bits = len(row_chunks(rows, 2)), len(row_chunks(rows, 4))
    tile = hidden_units // 3 if hidden_units % 48 == 0 else hidden_units
    columns = 8 * LANES
    most = 2
    bf16, f32, dma = jnp.bfloat16, jnp.float32, pltpu.SemaphoreType.DMA
    anywhere = pl.BlockSpec(memory_space=pl.ANY)
    return pl.pallas_call(
        functools.partial(layer_kernel, chips, heads, experts, tile, columns, most),
        out_shape=jax.ShapeDtypeStruct((rows, width), bf16),
        in_specs=[full_vmem()] * 4 + [anywhere] * 2,
        out_specs=full_vmem(),
        scratch_shapes=[
            pltpu.VMEM((blocks, rows, padded), bf16),
            pltpu.VMEM((tokens, routes.shape[1]), f32),
            pltpu.VMEM((LANES, width), bf16),
            pltpu.VMEM((2, hidden_units, width), bf16),
            pltpu.VMEM((hidden_units, width), bf16),
            pltpu.VMEM((hidden_units // tile, most * CORES * rows, tile), bf16),
            pltpu.VMEM((blocks, rows, width), bf16),
            pltpu.VMEM((2 * half, rows, width), bf16),
            pltpu.VMEM((2, half, rows, width), bf16),
            pltpu.VMEM((2, half, rows, width), bf16),
            dma((3, hidden_units // tile)),
            dma((2, half, parts)),
            dma((2, half, parts)),
            dma((2 * half + 1, parts)),
            dma((2 * half + 1, parts)),
            dma((2 * half,)),
            dma((2 * half,)),
            dma((2, half, bits)),
            dma((2, half, bits)),
        ],
        compiler_params=pltpu.CompilerParams(
            collective_id=1, has_side_effects=True, vmem_limit_bytes=60 * 1024 * 1024
        ),
        name="norm_and_experts",
    )(
        residual,
        norm_gain,
        router.T,
        routes.T,
        jnp.swapaxes(w_gate_up[0], 1, 2),
        w_down[0],
    )


def body(
    queries,
    keys,
    values,
    sinks,
    segments,
    hidden_in,
    routes,
    w_out,
    norm_gain,
    router,
    w_gate_up,
    w_down,
):
    residual = attend(queries, keys, values, sinks, segments, hidden_in, w_out)
    return norm_and_experts(residual, norm_gain, router, routes, w_gate_up, w_down)


def solution(mesh):
    placed = (
        P(("group", "ctx"), "head"),
        P(("group", "ctx"), "head"),
        P(("group", "ctx"), "head"),
        P("head"),
        P("group"),
        P(("group", "ctx"), None),
        P(("group", "ctx"), None),
        P("head", None),
        P(),
        P(),
        P("ctx", None, None, "head"),
        P("ctx", "head", None),
    )
    return jax.shard_map(
        body,
        mesh=mesh,
        in_specs=placed,
        out_specs=P(("group", "ctx", "head"), None),
        check_vma=False,
    )
```

```python
import functools
import math

import jax
import jax.numpy as jnp
from jax import lax
from jax.experimental import pallas as pl
from jax.experimental.pallas import tpu as pltpu
from jax.sharding import PartitionSpec as P

HEAD_SIZE = 64


masked_value = -1e30


MESH = pl.DeviceIdType.MESH
LANES = 128
CORES = 2


def full_vmem():
    return pl.BlockSpec(memory_space=pltpu.VMEM)


class Ring:
    def __init__(self, chips, heads):
        self.chips, self.heads, self.count = chips, heads, chips * heads
        ctx = lax.axis_index("ctx")
        self.head = lax.axis_index("head")
        self.core = lax.rem(ctx, CORES)
        z = lax.div(ctx, CORES)
        self.place = self.head * chips + z + lax.rem(self.head, 2) * (chips - 1 - 2 * z)
        self.partner = {"ctx": z * CORES + 1 - self.core, "head": self.head}

    def at(self, offset):
        spot = lax.rem(self.place + offset + self.count, self.count)
        head = lax.div(spot, self.chips)
        step = lax.rem(spot, self.chips)
        return head, step + lax.rem(head, 2) * (self.chips - 1 - 2 * step)

    def block(self, offset, core):
        head, z = self.at(offset)
        return (z * CORES + core) * self.heads + head

    def device(self, offset):
        head, z = self.at(offset)
        return {"ctx": z * CORES + self.core, "head": head}


def remote(src, dst, send_sem, recv_sem, device):
    return pltpu.make_async_remote_copy(
        src_ref=src, dst_ref=dst, send_sem=send_sem, recv_sem=recv_sem, device_id=device, device_id_type=MESH
    )


def row_chunks(rows, most):
    count = most if rows % (16 * most) == 0 else 1
    return [pl.ds(first, rows // count) for first in range(0, rows, rows // count)]


def attend_kernel(
    chips, heads, key_ref, value_ref, query_ref, sink_ref, segment_ref, hidden_ref, weight_hbm, out_ref,
    all_keys, all_values, stacked, group_keys, group_values, bias_ref, score_ref, peak_ref, attended_ref, weight_ref,
    hidden_rows, part_ref, slots,
    line_send, line_recv, pair_send, pair_recv, head_send, head_recv, weight_sem,
):
    ctx, head = lax.axis_index("ctx"), lax.axis_index("head")
    z, core = lax.div(ctx, CORES), lax.rem(ctx, CORES)
    rows = query_ref.shape[0]
    groups = key_ref.shape[1] // HEAD_SIZE
    share = query_ref.shape[1] // key_ref.shape[1]
    keys = CORES * rows
    own_rows, width = out_ref.shape
    ins, alls = (key_ref, value_ref), (all_keys, all_values)
    turned = (((1,), (1,)), ((), ()))
    partner = {"ctx": z * CORES + 1 - core}
    above = {"ctx": (z + 1) * CORES + core}
    others = [{"ctx": ctx, "head": lax.rem(head + turn, heads)} for turn in range(1, heads)]
    has_above, has_below = z + 1 < chips, z > 0
    load = pltpu.make_async_copy(weight_hbm, weight_ref, weight_sem)
    load.start()

    barrier = pltpu.get_barrier_semaphore()
    for device in [partner] + others:
        pl.semaphore_signal(barrier, inc=1, device_id=device, device_id_type=MESH)

    @pl.when(has_above)
    def _():
        pl.semaphore_signal(barrier, inc=1, device_id=above, device_id_type=MESH)

    @pl.when(has_below)
    def _():
        pl.semaphore_signal(barrier, inc=1, device_id={"ctx": (z - 1) * CORES + core}, device_id_type=MESH)

    peers = heads + jnp.where(has_above, 1, 0) + jnp.where(has_below, 1, 0)
    pl.semaphore_wait(barrier, peers)

    def hop(step, part):
        block = (z - step) * CORES + core
        source = ins[part] if step == 0 else alls[part].at[block]
        return remote(source, alls[part].at[block], line_send.at[step, part], line_recv.at[step, part], above)

    def relay(step, part):
        block = (z - step) * CORES + core
        source = ins[part] if step == 0 else alls[part].at[block]
        return remote(source, alls[part].at[block], pair_send.at[step, part], pair_recv.at[step, part], partner)

    for part in (0, 1):

        @pl.when(has_above)
        def _():
            hop(0, part).start()

        relay(0, part).start()
    for part in (0, 1):
        alls[part][ctx] = ins[part][...]

    for index in range(groups * share):
        span = slice(index * HEAD_SIZE, (index + 1) * HEAD_SIZE)
        stacked[index // share, index % share * rows : (index % share + 1) * rows, :] = query_ref[:, span]
    lane = lax.broadcasted_iota(jnp.int32, group_values.shape[1:], 1)
    for group in range(groups):
        group_values[group] = (lane == HEAD_SIZE).astype(jnp.float32).astype(jnp.bfloat16)
    here = pl.ds(pl.multiple_of(ctx * rows, rows), rows)
    diagonal = lax.broadcasted_iota(jnp.int32, (rows, rows), 0) == lax.broadcasted_iota(jnp.int32, (rows, rows), 1)
    own_segment = jnp.sum(
        jnp.where(diagonal, segment_ref[:, here].astype(jnp.float32), 0.0), axis=1, keepdims=True
    )
    log2e = math.log2(math.e)
    factor = HEAD_SIZE ** (-0.5) * log2e

    def score(step):
        chip = z - step
        block = all_keys[pl.ds(chip * CORES, CORES)].reshape(keys, key_ref.shape[1])
        for group in range(groups):
            group_keys[group] = block[:, group * HEAD_SIZE : (group + 1) * HEAD_SIZE]
        spot = lax.broadcasted_iota(jnp.int32, (rows, keys), 1) + chip * keys
        place = lax.broadcasted_iota(jnp.int32, (rows, keys), 0) + ctx * rows
        segment = segment_ref[:, pl.ds(pl.multiple_of(chip * keys, keys), keys)].astype(jnp.float32)
        bias_ref[...] = jnp.where((spot <= place) & (segment == own_segment), 0.0, masked_value)

        def one(group, carry):
            scores = lax.dot_general(stacked[group], group_keys[group], turned, preferred_element_type=jnp.float32)
            scores = scores.reshape(share, rows, keys) * factor + bias_ref[...]
            span = pl.ds(group * share, share)
            score_ref[step, span] = scores
            peak = scores[:, :, :LANES]
            for first in range(LANES, keys, LANES):
                peak = jnp.maximum(peak, scores[:, :, first : first + LANES])
            peak_ref[span] = peak if step == 0 else jnp.maximum(peak_ref[span], peak)
            return carry

        lax.fori_loop(0, groups, one, 0, unroll=2)

    def take_values(step):
        relay(step, 1).wait_recv()
        block = all_values[pl.ds((z - step) * CORES, CORES)].reshape(keys, value_ref.shape[1])
        for group in range(groups):
            group_values[group, step * keys : (step + 1) * keys, :HEAD_SIZE] = block[
                :, group * HEAD_SIZE : (group + 1) * HEAD_SIZE
            ]

    hidden_rows[...] = hidden_ref[...].T
    relay(0, 0).wait_recv()
    score(0)
    for step in range(1, chips):

        @pl.when(z - step >= 0)
        def _():
            for part in (0, 1):
                hop(step - 1, part).wait_recv()
                if step < chips - 1:

                    @pl.when(has_above)
                    def _():
                        hop(step, part).start()

                relay(step, part).start()
            take_values(step - 1)
            relay(step, 0).wait_recv()
            score(step)

        @pl.when(z - step < 0)
        def _():
            @pl.when(z - step == -1)
            def _():
                take_values(step - 1)

            def blank(index, carry):
                score_ref[step, index] = jnp.full((rows, keys), masked_value, jnp.float32)
                return carry

            lax.fori_loop(0, groups * share, blank, 0)

    @pl.when(z == chips - 1)
    def _():
        take_values(chips - 1)

    own = pl.ds(pl.multiple_of(head * own_rows, own_rows), own_rows)

    def mix(couple, carry):
        group = lax.div(couple * 2, share)
        sinks, tops = [], []
        for member in range(2):
            sinks.append(sink_ref[couple * 2 + member] * log2e)
            peak = jnp.max(peak_ref[couple * 2 + member], axis=-1, keepdims=True)
            tops.append(jnp.maximum(peak, sinks[member]))
        mixed = jnp.zeros((2 * rows, LANES), jnp.float32)
        for step in range(chips):
            weights = jnp.concatenate(
                [
                    jnp.exp2(score_ref[step, couple * 2 + member] - tops[member]).astype(jnp.bfloat16)
                    for member in range(2)
                ],
                axis=0,
            )
            mixed = mixed + jnp.dot(
                weights, group_values[group, step * keys : (step + 1) * keys, :], preferred_element_type=jnp.float32
            )
        both = []
        for member in range(2):
            mine = mixed[member * rows : (member + 1) * rows]
            total = mine[:, HEAD_SIZE : HEAD_SIZE + 1] + jnp.exp2(sinks[member] - tops[member])
            both.append((mine[:, :HEAD_SIZE] / total).astype(jnp.bfloat16))
        span = pl.ds(pl.multiple_of(couple * 2 * HEAD_SIZE, 2 * HEAD_SIZE), 2 * HEAD_SIZE)
        attended_ref[:, span] = jnp.concatenate(both, axis=1)
        return carry

    lax.fori_loop(0, groups * share // 2, mix, 0, unroll=min(8, groups * share // 2))

    load.wait()
    spans = column_spans(part_ref.shape[1])
    part_ref[:, spans[-1][0] :] = jnp.zeros((rows, spans[-1][1]), part_ref.dtype)
    sends = {}
    for c, (first, size) in enumerate(spans):
        last = min(first + size, width)
        piece = lax.dot_general(
            attended_ref[...], weight_ref[first:last, :], turned, preferred_element_type=jnp.float32
        )
        part_ref[:, first:last] = piece.astype(jnp.bfloat16)
        for turn, device in enumerate(others):
            target = pl.ds(pl.multiple_of(device["head"] * own_rows, own_rows), own_rows)
            sends[turn, c] = remote(
                part_ref.at[target, pl.ds(first, size)],
                slots.at[turn, :, pl.ds(first, size)],
                head_send.at[turn, c],
                head_recv.at[turn, c],
                device,
            )
            sends[turn, c].start()
    for c, (first, size) in enumerate(spans):
        span = slice(first, min(first + size, width))
        total = hidden_rows[own, span].astype(jnp.float32) + part_ref[own, span].astype(jnp.float32)
        for turn in range(heads - 1):
            sends[turn, c].wait_recv()
            total = total + slots[turn, :, span].astype(jnp.float32)
        out_ref[:, span] = total.astype(jnp.bfloat16)

    for copy in sends.values():
        copy.wait_send()
    for part in (0, 1):
        for step in range(chips):

            @pl.when(z - step >= 0)
            def _():
                relay(step, part).wait_send()
                if step < chips - 1:

                    @pl.when(has_above)
                    def _():
                        hop(step, part).wait_send()


def column_spans(padded):
    wide = 2 * LANES
    return [(first, min(wide, padded - first)) for first in range(0, padded, wide)]


def attend(queries, keys, values, sinks, segments, hidden, w_out):
    chips, heads = lax.axis_size("ctx") // CORES, lax.axis_size("head")
    n_ctx = lax.axis_size("ctx")
    rows = queries.shape[0]
    width = w_out.shape[1]
    padded = -(-width // LANES) * LANES
    groups = keys.shape[1] // HEAD_SIZE
    share = queries.shape[1] // keys.shape[1]
    parts = len(column_spans(padded))
    bf16, f32, dma = jnp.bfloat16, jnp.float32, pltpu.SemaphoreType.DMA
    chip_keys = CORES * rows
    return pl.pallas_call(
        functools.partial(attend_kernel, chips, heads),
        out_shape=jax.ShapeDtypeStruct((rows // heads, width), bf16),
        in_specs=[full_vmem()] * 3
        + [pl.BlockSpec(memory_space=pltpu.SMEM)]
        + [full_vmem()] * 2
        + [pl.BlockSpec(memory_space=pl.ANY)],
        out_specs=full_vmem(),
        scratch_shapes=[
            pltpu.VMEM((n_ctx,) + keys.shape, bf16),
            pltpu.VMEM((n_ctx,) + keys.shape, bf16),
            pltpu.VMEM((groups, share * rows, HEAD_SIZE), bf16),
            pltpu.VMEM((groups, chip_keys, HEAD_SIZE), bf16),
            pltpu.VMEM((groups, chips * chip_keys, LANES), bf16),
            pltpu.VMEM((rows, chip_keys), f32),
            pltpu.VMEM((chips, groups * share, rows, chip_keys), f32),
            pltpu.VMEM((groups * share, rows, LANES), f32),
            pltpu.VMEM(queries.shape, bf16),
            pltpu.VMEM((width, w_out.shape[0]), bf16),
            pltpu.VMEM((rows, width), bf16),
            pltpu.VMEM((rows, padded), bf16),
            pltpu.VMEM((heads - 1, rows // heads, padded), bf16),
            dma((chips, 2)),
            dma((chips, 2)),
            dma((chips, 2)),
            dma((chips, 2)),
            dma((heads - 1, parts)),
            dma((heads - 1, parts)),
            dma(()),
        ],
        compiler_params=pltpu.CompilerParams(
            collective_id=0, has_side_effects=True, vmem_limit_bytes=60 * 1024 * 1024
        ),
        name="attend",
    )(keys, values, queries, sinks, segments.reshape(1, -1), hidden.T, w_out.T)


def layer_kernel(
    chips, heads, experts, tile, columns, most, residual_ref, gain_ref, router_ref, route_ref, up_hbm, down_hbm,
    out_ref, all_ref, route_rows, lanes_ref, up_ref, down_ref, act_ref, term_ref, got, outgoing, incoming, weight_sem,
    hop_send, hop_recv, copy_send, copy_recv, pair_send, pair_recv, ring_send, ring_recv,
):
    ring = Ring(chips, heads)
    count, half = ring.count, ring.count // 2
    rows, width = out_ref.shape
    start = width % LANES
    chunks, bits = row_chunks(rows, 2), row_chunks(rows, 4)
    parts = range(len(chunks))
    depth = len(bits) // len(chunks)
    order = [part * depth + j for j in range(depth) for part in parts]
    ways = ((0, 1), (1, -1))
    turned = (((1,), (1,)), ((), ()))
    ctx, head = lax.axis_index("ctx"), ring.head

    barrier = pltpu.get_barrier_semaphore()
    peers = [ring.device(1), ring.device(-1), ring.partner]
    for device in peers:
        pl.semaphore_signal(barrier, inc=1, device_id=device, device_id_type=MESH)
    tiles = act_ref.shape[0]

    def load_up(t):
        span = pl.ds(pl.multiple_of(t * tile, 8), tile)
        return [
            pltpu.make_async_copy(up_hbm.at[which, span], up_ref.at[which, span], weight_sem.at[which, t])
            for which in range(2)
        ]

    load_down = pltpu.make_async_copy(down_hbm, down_ref, weight_sem.at[2, 0])
    for t in range(tiles):
        for copy in load_up(t):
            copy.start()
    load_down.start()

    own = pl.ds(pl.multiple_of(head * rows, rows), rows)
    tokens = route_ref.shape[1]
    eye = (
        lax.broadcasted_iota(jnp.int32, (tokens, tokens), 0) == lax.broadcasted_iota(jnp.int32, (tokens, tokens), 1)
    ).astype(jnp.float32)
    route_rows[...] = lax.dot_general(
        eye.astype(jnp.bfloat16),
        route_ref[...].astype(jnp.float32).astype(jnp.bfloat16),
        turned,
        preferred_element_type=jnp.float32,
    )
    lanes_ref[...] = jnp.zeros(lanes_ref.shape, lanes_ref.dtype)
    lanes_ref[start : start + experts, :] = router_ref[...]
    lanes_ref[start + experts : start + 2 * experts, :] = router_ref[...]

    residual = residual_ref[...]
    wide = residual.astype(jnp.float32)
    scale = lax.rsqrt(jnp.mean(wide * wide, axis=-1, keepdims=True) + 1e-05)
    normed = (wide * scale * gain_ref[...][None, :]).astype(jnp.bfloat16)

    logits = lax.dot_general(normed, lanes_ref[...], turned, preferred_element_type=jnp.float32)
    lane = lax.broadcasted_iota(jnp.int32, logits.shape, 1) - start
    first = (lane >= 0) & (lane < experts)
    names = route_rows[own, :]
    present = jnp.zeros(logits.shape, jnp.bool_)
    spot = lane.astype(jnp.float32)
    for k in range(route_ref.shape[0]):
        name = names[:, k : k + 1]
        present = present | (spot == name) | (spot - experts == name)
    top = jnp.max(jnp.where(present, logits, -jnp.inf), axis=-1, keepdims=True)
    powers = jnp.where(present, jnp.exp(jnp.where(present, logits - top, 0.0)), 0.0)
    gates = powers / jnp.sum(jnp.where(first, powers, 0.0), axis=-1, keepdims=True)
    coarse = gates.astype(jnp.bfloat16)
    rest = gates - coarse.astype(jnp.float32)
    tail = jnp.where(first, coarse.astype(jnp.float32), rest)
    mine = ring.block(0, ring.core)
    all_ref[mine, :, width - start :] = tail.astype(jnp.bfloat16)
    all_ref[mine, :, :width] = normed

    def last(index, j):
        return (j == 0) == (index == 0)

    def hop(index, way, step, j):
        view = all_ref.at[ring.block(-way * step, ring.core), chunks[j]]
        return remote(view, view, hop_send.at[index, step, j], hop_recv.at[index, step, j], ring.device(way))

    def relay(slot, offset, j):
        view = all_ref.at[ring.block(offset, ring.core), chunks[j]]
        return remote(view, view, copy_send.at[slot, j], copy_recv.at[slot, j], ring.partner)

    def continues(index, step, j):
        return step < half - 1 or (step == half - 1 and last(index, j))

    def forward(step, j):
        for index, way in ways:
            if continues(index, step - 1, j):
                hop(index, way, step - 1, j).wait_recv()
                if continues(index, step, j):
                    hop(index, way, step, j).start()
                relay(index * half + step, -way * step, j).start()

    def slot_of(offset):
        return offset + half if 0 < offset < half else abs(offset)

    def share(offset):
        slot = slot_of(offset)
        return remote(
            term_ref.at[ring.block(offset, 1 - ring.core)], got.at[slot], pair_send.at[slot], pair_recv.at[slot], ring.partner
        )

    def multiply_blocks(offsets, hooks, fresh):
        blocks = [ring.block(offset, core) for offset in offsets for core in range(CORES)]
        used = len(blocks) * rows
        gates = []
        for block in blocks:
            tail = all_ref[block, :, width - start :].astype(jnp.float32)
            lane = lax.broadcasted_iota(jnp.int32, tail.shape, 1) - start
            here = (lane == ctx) | (lane == ctx + experts)
            gates.append(jnp.sum(jnp.where(here, tail, 0.0), axis=1, keepdims=True))
        gate = jnp.concatenate(gates, axis=0)

        def multiply(t, carry):
            if fresh:
                for copy in load_up(t):
                    copy.wait()
            span = pl.ds(pl.multiple_of(t * tile, 8), tile)
            x = jnp.concatenate([all_ref[block, :, :width] for block in blocks], axis=0)
            a = lax.dot_general(x, up_ref[0, span, :], turned, preferred_element_type=jnp.float32)
            b = lax.dot_general(x, up_ref[1, span, :], turned, preferred_element_type=jnp.float32)
            act_ref[t, :used, :] = (a * jax.nn.sigmoid(1.702 * a) * (b + 1.0)).astype(jnp.bfloat16)
            for spot in range(3):
                if hooks[spot]:

                    @pl.when(t == min(spot, tiles - 1))
                    def _():
                        for hook in hooks[spot]:
                            hook()

            return carry

        lax.fori_loop(0, tiles, multiply, 0)
        if fresh:
            load_down.wait()
        for first in range(0, width, columns):
            span = slice(first, min(first + columns, width))
            piece = 0.0
            for t in range(tiles):
                piece = piece + jnp.dot(
                    act_ref[t, :used, :], down_ref[t * tile : (t + 1) * tile, span], preferred_element_type=jnp.float32
                )
            gated = (piece * gate).astype(jnp.bfloat16)
            for i, block in enumerate(blocks):
                term_ref[block, :, span] = gated[i * rows : (i + 1) * rows]
            if first == columns:
                for hook in hooks[3]:
                    hook()

    def experts_on(offsets, hooks=((), (), (), ()), fresh=False):
        for offset in offsets:
            for index, way in ways:
                for j in parts:
                    distance = abs(offset)
                    if offset == 0:
                        if index == 0:
                            relay(0, 0, j).wait_recv()
                    elif continues(index, distance - 1, j) and (distance == half or offset == -way * distance):
                        relay(index * half + distance, -way * distance, j).wait_recv()
        for first in range(0, len(offsets), most):
            multiply_blocks(offsets[first : first + most], hooks, fresh)
            hooks, fresh = ((), (), (), ()), False
        for offset in offsets:
            share(offset).start()

    arrived = set()

    def pair(offset, bit):
        offset = half if offset == -half else offset
        if offset not in arrived:
            share(offset).wait_recv()
            arrived.add(offset)
        mine = term_ref[ring.block(offset, ring.core), bits[bit], :].astype(jnp.float32)
        return mine + got[slot_of(offset), bits[bit], :].astype(jnp.float32)

    def travelling(index, way, step, bit):
        return remote(
            outgoing.at[index, step, bits[bit]],
            incoming.at[index, step, bits[bit]],
            ring_send.at[index, step, bit],
            ring_recv.at[index, step, bit],
            ring.device(way),
        )

    def ring_step(final, step, bit):
        for index, way in ways:
            if last(index, bit // depth) == final:
                total = pair(way * (half - step), bit)
                if step > (0 if final else 1):
                    travelling(index, way, step - 1, bit).wait_recv()
                    total = total + incoming[index, step - 1, bits[bit], :].astype(jnp.float32)
                outgoing[index, step, bits[bit], :] = total.astype(jnp.bfloat16)
                travelling(index, way, step, bit).start()

    def finish(bit):
        total = pair(0, bit) + residual_ref[bits[bit], :].astype(jnp.float32)
        for index, way in ways:
            travelling(index, way, half - 1, bit).wait_recv()
            total = total + incoming[index, half - 1, bits[bit], :].astype(jnp.float32)
        out_ref[bits[bit], :] = total.astype(jnp.bfloat16)

    def gather(step, j):
        return functools.partial(forward, step, j)

    def short(step, bit):
        return functools.partial(ring_step, False, step, bit)

    pl.semaphore_wait(barrier, len(peers))
    for j in parts:
        for index, way in ways:
            if continues(index, 0, j):
                hop(index, way, 0, j).start()
        relay(0, 0, j).start()
    if depth == 2 and half == 4:
        experts_on([0], ((), (), [gather(1, 0)], ()), fresh=True)
        forward(1, 1)
        experts_on([1, -1], ((), [gather(2, 0)], (), [gather(2, 1)]))
        experts_on([2, -2], ((), [gather(3, 0)], (), [gather(3, 1)]))
        experts_on([3, -3], ((), [gather(4, 0), gather(4, 1)], (), ()))
        for bit in order:
            ring_step(False, 1, bit)
        experts_on([4], ((), [short(2, 0), short(2, 2)], [short(2, 1), short(2, 3)], ()))
        for bit in order:
            ring_step(True, 0, bit)
        for bit in order:
            ring_step(False, 3, bit)
        for step in (1, 2, 3):
            for bit in order:
                ring_step(True, step, bit)
    else:
        for step in range(1, half + 1):
            for j in parts:
                forward(step, j)
        offsets = [0]
        for distance in range(1, half):
            offsets += [distance, -distance]
        experts_on(offsets + [half], fresh=True)
        for step in range(half):
            for bit in order:
                ring_step(True, step, bit)
                if step > 0:
                    ring_step(False, step, bit)
    for bit in order:
        finish(bit)

    for offset in range(1 - half, half + 1):
        share(offset).wait_send()
    for j in parts:
        relay(0, 0, j).wait_send()
    for index, way in ways:
        for step in range(half):
            for j in parts:
                if continues(index, step, j):
                    hop(index, way, step, j).wait_send()
                    relay(index * half + step + 1, -way * (step + 1), j).wait_send()
            for bit in order:
                if step > 0 or last(index, bit // depth):
                    travelling(index, way, step, bit).wait_send()


def norm_and_experts(residual, norm_gain, router, routes, w_gate_up, w_down):
    chips, heads = lax.axis_size("ctx") // CORES, lax.axis_size("head")
    rows, width = residual.shape
    tokens = rows * heads
    experts = router.shape[1]
    hidden_units = w_down.shape[1]
    padded = width - width % LANES + LANES
    half = chips * heads // 2
    blocks = chips * heads * CORES
    parts, bits = len(row_chunks(rows, 2)), len(row_chunks(rows, 4))
    tile = hidden_units // 3 if hidden_units % 48 == 0 else hidden_units
    columns = 8 * LANES
    most = 2
    bf16, f32, dma = jnp.bfloat16, jnp.float32, pltpu.SemaphoreType.DMA
    anywhere = pl.BlockSpec(memory_space=pl.ANY)
    return pl.pallas_call(
        functools.partial(layer_kernel, chips, heads, experts, tile, columns, most),
        out_shape=jax.ShapeDtypeStruct((rows, width), bf16),
        in_specs=[full_vmem()] * 4 + [anywhere] * 2,
        out_specs=full_vmem(),
        scratch_shapes=[
            pltpu.VMEM((blocks, rows, padded), bf16),
            pltpu.VMEM((tokens, routes.shape[1]), f32),
            pltpu.VMEM((LANES, width), bf16),
            pltpu.VMEM((2, hidden_units, width), bf16),
            pltpu.VMEM((hidden_units, width), bf16),
            pltpu.VMEM((hidden_units // tile, most * CORES * rows, tile), bf16),
            pltpu.VMEM((blocks, rows, width), bf16),
            pltpu.VMEM((2 * half, rows, width), bf16),
            pltpu.VMEM((2, half, rows, width), bf16),
            pltpu.VMEM((2, half, rows, width), bf16),
            dma((3, hidden_units // tile)),
            dma((2, half, parts)),
            dma((2, half, parts)),
            dma((2 * half + 1, parts)),
            dma((2 * half + 1, parts)),
            dma((2 * half,)),
            dma((2 * half,)),
            dma((2, half, bits)),
            dma((2, half, bits)),
        ],
        compiler_params=pltpu.CompilerParams(
            collective_id=1, has_side_effects=True, vmem_limit_bytes=60 * 1024 * 1024
        ),
        name="norm_and_experts",
    )(
        residual,
        norm_gain,
        router.T,
        routes.T,
        jnp.swapaxes(w_gate_up[0], 1, 2),
        w_down[0],
    )


def body(
    queries,
    keys,
    values,
    sinks,
    segments,
    hidden_in,
    routes,
    w_out,
    norm_gain,
    router,
    w_gate_up,
    w_down,
):
    residual = attend(queries, keys, values, sinks, segments, hidden_in, w_out)
    return norm_and_experts(residual, norm_gain, router, routes, w_gate_up, w_down)


def solution(mesh):
    placed = (
        P(("group", "ctx"), "head"),
        P(("group", "ctx"), "head"),
        P(("group", "ctx"), "head"),
        P("head"),
        P("group"),
        P(("group", "ctx"), None),
        P(("group", "ctx"), None),
        P("head", None),
        P(),
        P(),
        P("ctx", None, None, "head"),
        P("ctx", "head", None),
    )
    return jax.shard_map(
        body,
        mesh=mesh,
        in_specs=placed,
        out_specs=P(("group", "ctx", "head"), None),
        check_vma=False,
    )
```
